32 devices in a mesh: flow: 8 (over z, x), lat: 4 (over y, core).
Axes of the slice: x: 2, y: 2, z: 4, core: 2. Of those that a mesh axis runs over, the one named last changes fastest.
Arguments:
- conc_old: float32 [2, 64, 64, 2048], P(None, 'flow', None, 'lat'), may hold values from -6 to 6
- lat_velocity: float32 [64, 2048], P('flow', 'lat'), may hold values from -3 to 3
- elem_type: int32 [64, 2048], P('flow', 'lat'), may hold values from 0 to 3
- inlet_trace: float32 [2, 16, 2048], P(None, None, 'lat'), may hold values from -6 to 6
- solve_table: float32 [2, 4, 64, 80], replicated, may hold values from -0.65 to 1.25
Outputs:
- conc_new: bfloat16 [2, 64, 64, 2048], P(None, 'flow', None, 'lat')
The draws below stay inside these ranges and needn't reach their ends.
All inputs are finite; a program needn't handle non-finite values.
Results may differ from the reference program's by a relative error of at most 0.001.
Values sent between devices are 32-bit elements; how exact they have to be, the bound alone decides.
No kernel may reach another device: no remote copies, remote signals or barrier semaphores. Data moves between devices by JAX's collectives and lax.ppermute only.
A program may use at most 64 MiB of HBM per device.

```python
import jax
import jax.numpy as jnp
from jax import lax

SPECIES = 2
DOF = 64
TRACE = 16
NTYPE = 4
NL = 64
NCOLS = 2048


def draw_solve_table(key, part):
    keys = jax.random.split(key, 5)
    table_shape = (SPECIES, NTYPE, DOF, DOF + TRACE)
    noise_draw = jnp.clip(jax.random.normal(keys[0], table_shape, jnp.float32), -4.0, 4.0)
    row_index = jax.lax.broadcasted_iota(jnp.int32, table_shape, 2)
    col_index = jax.lax.broadcasted_iota(jnp.int32, table_shape, 3)
    diagonal = jax.random.uniform(keys[1], table_shape, jnp.float32, 0.5, 1.0)
    interior_part = jnp.where(row_index == col_index, diagonal, 0.0) + 0.05 * noise_draw
    interior_part = jnp.where(row_index >= DOF - TRACE, 0.1 * interior_part, interior_part)
    slow_mask = jax.random.uniform(keys[2], (SPECIES, 1, DOF, 1), jnp.float32) < 0.5
    slow_decay = jax.random.uniform(keys[3], table_shape, jnp.float32, 0.996, 0.9995)
    fast_decay = jax.random.uniform(keys[4], table_shape, jnp.float32, 0.3, 0.9)
    decay_rate = jnp.where(slow_mask, slow_decay, fast_decay)
    coupling_col = col_index - DOF
    channel = row_index - (DOF - TRACE)
    top_rows = jnp.where(coupling_col == channel, decay_rate, jnp.where(coupling_col < channel, 0.02 * noise_draw, 0.0))
    coupling_part = jnp.where(row_index >= DOF - TRACE, top_rows, 0.15 * noise_draw)
    return jnp.where(col_index < DOF, interior_part, coupling_part).astype(jnp.float32)


def place_ends(array, own_key, low, top_value):
    dims = array.shape
    place = [jax.random.randint(jax.random.fold_in(own_key, axis), (), 0, dims[axis]) for axis in range(len(dims))]
    array = array.at[tuple(place)].set(low)
    longest = dims.index(max(dims))
    place[longest] = (place[longest] + 1) % dims[longest]
    return array.at[tuple(place)].set(top_value)


def shard_levels(rng, shape, pieces, least, largest):
    level = 1.0
    for dim, shards_of in pieces:
        draws = jax.random.uniform(jax.random.fold_in(jax.random.fold_in(rng, 6), dim), (shards_of,), jnp.float32, least / len(pieces), largest / len(pieces))
        level = level * jnp.repeat(jnp.exp(draws), shape[dim] // shards_of).reshape((-1,) + (1,) * (len(shape) - 1 - dim))
    return level


def gaussian(stream_key, extent, scale, limit, pieces=(), kind=jnp.bfloat16):
    loudness = shard_levels(stream_key, extent, pieces, -0.22, 0.18) if pieces else 1.0
    values = jax.random.normal(stream_key, extent, jnp.float32) * scale * loudness
    return jnp.minimum(jnp.maximum(values, -limit), limit).astype(kind)


def setup_inputs(seed: int = 0) -> dict:
    key_list = jax.random.split(jax.random.key(seed), 6)
    return {
        "conc_old": gaussian(key_list[0], (SPECIES, NL, DOF, NCOLS), 1.0, 6.0, ((1, 8), (3, 4)), jnp.float32),
        "lat_velocity": gaussian(key_list[1], (NL, NCOLS), 0.5, 3.0, ((0, 8), (1, 4)), jnp.float32),
        "elem_type": place_ends(jax.random.randint(key_list[2], (NL, NCOLS), 0, NTYPE), jax.random.fold_in(key_list[2], 1), 0, NTYPE - 1).astype(jnp.int32),
        "inlet_trace": gaussian(key_list[3], (SPECIES, TRACE, NCOLS), 1.0, 6.0, ((2, 4),), jnp.float32),
        "solve_table": draw_solve_table(jax.random.fold_in(key_list[5], 71), 0),
    }


precise = lax.Precision.HIGHEST


def add_faces(conc_old, flux_left, flux_right):
    shp = conc_old.shape
    dof_grid = conc_old.reshape(shp[0], shp[1], shp[2] // 4, 4, shp[3])
    dof_grid = dof_grid.at[:, :, :, 0, :].add(flux_left)
    dof_grid = dof_grid.at[:, :, :, 3, :].add(-flux_right)
    return dof_grid.reshape(shp)


def reference(conc_old, lat_velocity, elem_type, inlet_trace, solve_table):
    right_tr = conc_old[:, :, 3::4, :]
    left_tr = conc_old[:, :, 0::4, :]
    zero_rim = jnp.zeros_like(right_tr[..., :1])
    upwind = jnp.concatenate([zero_rim, right_tr[..., :-1]], axis=3)
    velocity = lat_velocity[None, :, None, :]
    flux_left = jnp.maximum(velocity, 0.0) * upwind + jnp.minimum(velocity, 0.0) * left_tr
    flux_right = jnp.concatenate([flux_left[..., 1:], zero_rim], axis=3)
    source = add_faces(conc_old, flux_left, flux_right)
    type_count = solve_table.shape[1]
    type_ids = jnp.arange(type_count, dtype=jnp.int32)
    trace_size = inlet_trace.shape[1]

    def level_step(trace_in, inputs_level):
        source_level, type_level = inputs_level
        onehot = (type_level[None, :] == type_ids[:, None]).astype(jnp.float32)
        stacked = jnp.concatenate([source_level, trace_in], axis=1)
        per_type = jnp.einsum('stij,sjc->stic', solve_table, stacked, precision=precise)
        solved = jnp.einsum('tc,stic->sic', onehot, per_type, precision=precise)
        return solved[:, -trace_size:, :], solved

    final_trace, solved_levels = lax.scan(level_step, inlet_trace, (jnp.moveaxis(source, 1, 0), elem_type))
    return jnp.moveaxis(solved_levels, 0, 1).astype(jnp.bfloat16)
```

```python
import functools

import jax
import jax.numpy as jnp
from jax import lax
from jax.experimental import pallas as pl
from jax.experimental.pallas import tpu as pltpu
from jax.sharding import PartitionSpec as P

F32 = jnp.float32
BF16 = jnp.bfloat16
VMEM = pl.BlockSpec(memory_space=pltpu.VMEM)
ANY = pl.BlockSpec(memory_space=pl.ANY)


def lane_index(shape):
    return lax.broadcasted_iota(jnp.int32, shape, len(shape) - 1)


def split(x):
    hi = x.astype(BF16)
    return hi, (x - hi.astype(F32)).astype(BF16)


def stacked_parts(x):
    hi, lo = split(x)
    return jnp.concatenate([hi, lo, hi], axis=0)


def pick(per_type, types, rows):
    count = per_type.shape[0] // rows
    out = per_type[:rows]
    for t in range(1, count):
        out = jnp.where(types == t, per_type[t * rows : (t + 1) * rows], out)
    return out


def mm(a, b):
    return jnp.dot(a, b, preferred_element_type=F32)


def local_kernel(
    conc_hbm, vel_ref, type_ref, table_ref, s_ref, inner_ref, couple_ref, x_ref, sems
):
    species, levels, dofs, columns = x_ref.shape
    copies = []
    for s in range(species):
        for l in range(levels):
            k = s * levels + l
            copies.append(pltpu.make_async_copy(conc_hbm.at[s, l], x_ref.at[s, l], sems.at[k]))
            copies[-1].start()
    types_n, lanes = table_ref.shape[1], table_ref.shape[3]
    trace = couple_ref.shape[2] // 3
    for s in range(species):
        table = table_ref[s].reshape(types_n * dofs, lanes)
        hi = table.astype(BF16).astype(F32)
        lo = table - hi
        lane = lane_index(table.shape)
        twice = jnp.where(lane < dofs, hi, pltpu.roll(hi, dofs, 1))
        inner_ref[s] = jnp.concatenate([twice, lo[:, :dofs]], axis=1).astype(BF16)
        first = pltpu.roll(hi, lanes - dofs, 1)
        second = pltpu.roll(hi, lanes - dofs + trace, 1)
        third = pltpu.roll(lo, lanes - dofs + 2 * trace, 1)
        joined = jnp.where(lane < trace, first, jnp.where(lane < 2 * trace, second, third))
        couple_ref[s] = joined[:, : 3 * trace].astype(BF16)
    row = lax.broadcasted_iota(jnp.int32, (8, columns), 0) % 4
    lane = lane_index((8, columns))
    for l in range(levels):
        velocity = jnp.broadcast_to(vel_ref[l : l + 1], (8, columns))
        following = pltpu.roll(velocity, columns - 1, 1)
        following = jnp.where(lane == columns - 1, 0.0, following)
        own = 1.0 + jnp.where(
            row == 0,
            jnp.minimum(velocity, 0.0),
            jnp.where(row == 3, -jnp.maximum(following, 0.0), 0.0),
        )
        left = jnp.where((row == 0) & (lane > 0), jnp.maximum(velocity, 0.0), 0.0)
        right = jnp.where(row == 3, -jnp.minimum(following, 0.0), 0.0)
        types = type_ref[l : l + 1]
        for s in range(species):
            copies[s * levels + l].wait()
            x = x_ref[s, l].reshape(dofs // 8, 8, columns)
            up = pltpu.roll(pltpu.roll(x, 1, 2), 5, 1)
            down = pltpu.roll(pltpu.roll(x, columns - 1, 2), 3, 1)
            source = own[None] * x + left[None] * up + right[None] * down
            parts = stacked_parts(source.reshape(dofs, columns))
            s_ref[s, l] = pick(mm(inner_ref[s], parts), types, dofs)


def edge_kernel(
    top_rows, s_ref, type_ref, vel_ref, inlet_ref, inner_ref, couple_ref, own_ref, left_ref, right_ref,
    corr_ref, send_ref,
):
    species, levels, dofs, columns = s_ref.shape
    trace = inlet_ref.shape[1]
    pairs = species * levels
    types_n = inner_ref.shape[1] // dofs
    lat, lat_n = lax.axis_index("lat"), lax.axis_size("lat")
    has_left = (lat > 0).astype(F32)
    has_right = (lat < lat_n - 1).astype(F32)
    rim, nxt = left_ref[...] * has_left, right_ref[...] * has_right
    own_last = own_ref[pairs:]
    lanes = rim.shape[1]
    lane = lane_index(rim.shape)
    inside = lane < dofs
    own_vel = pltpu.roll(own_ref[:pairs], dofs, 1)
    nxt_vel = pltpu.roll(nxt, dofs, 1)
    first = jnp.where(
        inside & (lane % 4 == 0), jnp.maximum(own_vel, 0.0) * pltpu.roll(rim, lanes - 3, 1), 0.0
    )
    last = jnp.where(
        inside & (lane % 4 == 3),
        -(jnp.maximum(nxt_vel, 0.0) * own_last + jnp.minimum(nxt_vel, 0.0) * pltpu.roll(nxt, 3, 1)),
        0.0,
    )
    sub = lax.broadcasted_iota(jnp.int32, (levels, lanes), 0)
    on_diag = lane_index((levels, lanes)) % levels == sub
    types = type_ref[...]
    contract = (((1,), (1,)), ((), ()))
    for e, (delta, col) in enumerate(((first, 0), (last, columns - 1))):
        hi = delta.astype(BF16).astype(F32)
        lo = delta - hi
        parts = jnp.concatenate(
            [jnp.where(inside, hi, pltpu.roll(lo, dofs, 1)), hi[:, :dofs]], axis=1
        ).astype(BF16)
        edge_type = jnp.broadcast_to(types[:, col : col + 1], (levels, lanes))
        edge_type = jnp.sum(jnp.where(on_diag, edge_type, 0), axis=0, keepdims=True)[:, :pairs]
        for s in range(species):
            per_type = lax.dot_general(inner_ref[s], parts, contract, preferred_element_type=F32)
            corr_ref[e, s, :, :pairs] = pick(per_type, edge_type, dofs)
    flow = lax.axis_index("flow")
    start = (flow == 0).astype(F32)
    traces = [inlet_ref[s] * start for s in range(species)]
    for l in range(levels):
        tl = types[l : l + 1]
        for s in range(species):
            moved = pick(mm(top_rows(couple_ref, s), stacked_parts(traces[s])), tl, trace)
            fixed = edge_fix(corr_ref, s, l, levels, dofs - trace, trace, columns)
            traces[s] = moved + s_ref[s, l, dofs - trace :] + fixed
    width = send_ref.shape[2]
    if width == 128:
        half = width // 2
        low = lane_index((trace, width)) < half
        low_t = lane_index((levels, width)) < half
        ftypes = types.astype(F32)
        for k in range(columns // width):
            a, b = (traces[s][:, k * width : (k + 1) * width] for s in (0, 1))
            t = ftypes[:, k * width : (k + 1) * width]
            swapped = pltpu.roll(t, half, 1)
            send_ref[2 * k, :trace] = jnp.where(low, a, pltpu.roll(b, half, 1))
            send_ref[2 * k + 1, :trace] = jnp.where(low, pltpu.roll(a, half, 1), b)
            send_ref[2 * k, trace:] = jnp.where(low_t, t, swapped)
            send_ref[2 * k + 1, trace:] = jnp.where(low_t, swapped, t)
    else:
        for s in range(species):
            send_ref[s, :trace] = traces[s]
            send_ref[s, trace:] = types.astype(F32)


def edge_fix(corr_ref, s, l, levels, start, rows, columns):
    at = s * levels + l
    lane = lane_index((rows, 128))
    first = pltpu.roll(corr_ref[0, s, start : start + rows], (128 - at) % 128, 1)
    last = pltpu.roll(corr_ref[1, s, start : start + rows], 127 - at, 1)
    first = jnp.where(lane == 0, first, 0.0)
    last = jnp.where(lane == 127, last, 0.0)
    middle = jnp.zeros((rows, columns - 256), F32)
    return jnp.concatenate([first, middle, last], axis=1)


def owner_kernel(table_ref, got_ref, out_ref, coef_ref):
    slabs, _, width = got_ref.shape
    species, types_n, trace, _ = table_ref.shape
    levels = got_ref.shape[1] - trace
    half = width // species
    which = lane_index((trace, width)) // half
    for t in range(types_n):
        for j in range(trace):
            value = jnp.broadcast_to(table_ref[0, t, :, j : j + 1], (trace, width))
            for s in range(1, species):
                other = jnp.broadcast_to(table_ref[s, t, :, j : j + 1], (trace, width))
                value = jnp.where(which == s, other, value)
            coef_ref[t, j] = value
    out_ref[0] = jnp.zeros((trace, width), F32)

    def slab(g, state):
        out_ref[g] = state
        for l in range(levels):
            types = jnp.broadcast_to(got_ref[g, trace + l : trace + l + 1], (trace, width))
            chosen = [types == float(t) for t in range(1, types_n)]
            terms = []
            for j in range(trace):
                coef = coef_ref[0, j]
                for t in range(1, types_n):
                    coef = jnp.where(chosen[t - 1], coef_ref[t, j], coef)
                terms.append(coef * state[j : j + 1])
            while len(terms) > 1:
                terms = [a + b for a, b in zip(terms[::2], terms[1::2])]
            state = terms[0]
        return state + got_ref[g, :trace]

    last = lax.fori_loop(1, slabs - 1, slab, got_ref[0, :trace])
    out_ref[slabs - 1] = last


def final_kernel(
    s_ref, type_ref, inlet_ref, couple_ref, corr_ref, got_ref, out_hbm, o_ref, sems
):
    species, levels, dofs, columns = s_ref.shape
    trace = inlet_ref.shape[1]
    width = got_ref.shape[2]
    is_first = lax.axis_index("flow") == 0
    traces = []
    if width == 128:
        half = width // 2
        low = lane_index((trace, width)) < half
        tiles = [[], []]
        for k in range(columns // width):
            a, b = got_ref[2 * k], got_ref[2 * k + 1]
            tiles[0].append(jnp.where(low, a, pltpu.roll(b, half, 1)))
            tiles[1].append(jnp.where(low, pltpu.roll(a, half, 1), b))
        received = [jnp.concatenate(t, axis=1) for t in tiles]
    else:
        received = [got_ref[s] for s in range(species)]
    traces = [jnp.where(is_first, inlet_ref[s], received[s]) for s in range(species)]
    copies = []
    for l in range(levels):
        types = type_ref[l : l + 1]
        for s in range(species):
            moved = pick(mm(couple_ref[s], stacked_parts(traces[s])), types, dofs)
            out = moved + s_ref[s, l] + edge_fix(corr_ref, s, l, levels, 0, dofs, columns)
            traces[s] = out[dofs - trace :]
            o_ref[s, l] = out.astype(BF16)
            copies.append(
                pltpu.make_async_copy(o_ref.at[s, l], out_hbm.at[s, l], sems.at[s * levels + l])
            )
            copies[-1].start()
    for copy in copies:
        copy.wait()


def on_device(conc_old, lat_velocity, elem_type, inlet_trace, solve_table):
    species, levels, dofs, columns = conc_old.shape
    types_n = solve_table.shape[1]
    trace = inlet_trace.shape[1]
    flow_n = lax.axis_size("flow")
    lat_n = lax.axis_size("lat")
    pairs = species * levels
    shape = jax.ShapeDtypeStruct

    face = jnp.broadcast_to(lat_velocity[None, :, :1], (species, levels, dofs)).reshape(pairs, dofs)
    first = jnp.concatenate([conc_old[:, :, :, 0].reshape(pairs, dofs), face], axis=1)
    last = jnp.concatenate([conc_old[:, :, :, columns - 1].reshape(pairs, dofs), face], axis=1)
    from_left = lax.ppermute(last, "lat", [(i, (i + 1) % lat_n) for i in range(lat_n)])
    from_right = lax.ppermute(first, "lat", [((i + 1) % lat_n, i) for i in range(lat_n)])
    own = jnp.concatenate([first, last], axis=0)

    table = jnp.pad(solve_table, ((0, 0), (0, 0), (0, 0), (0, 128 - dofs - trace)))
    source, inner, couple = pl.pallas_call(
        local_kernel,
        out_shape=(
            shape((species, levels, dofs, columns), F32),
            shape((species, types_n * dofs, 3 * dofs), BF16),
            shape((species, types_n * dofs, 3 * trace), BF16),
        ),
        in_specs=[ANY, VMEM, VMEM, VMEM],
        out_specs=(VMEM, VMEM, VMEM),
        scratch_shapes=[
            pltpu.VMEM((species, levels, dofs, columns), F32),
            pltpu.SemaphoreType.DMA((pairs,)),
        ],
        cost_estimate=pl.CostEstimate(
            flops=2 * 3 * types_n * dofs * dofs * columns * pairs,
            bytes_accessed=8 * species * levels * dofs * columns,
            transcendentals=0,
        ),
        name="local_sources",
    )(conc_old, lat_velocity, elem_type, table)

    packed = 2 * columns == 128 * flow_n and species == 2

    def top_rows(couple_ref, s):
        return jnp.concatenate(
            [couple_ref[s, (t + 1) * dofs - trace : (t + 1) * dofs] for t in range(types_n)], axis=0
        )

    send_shape = (flow_n, trace + levels, 128) if packed else (species, trace + levels, columns)
    corr, send = pl.pallas_call(
        functools.partial(edge_kernel, top_rows),
        out_shape=(shape((2, species, dofs, 128), F32), shape(send_shape, F32)),
        in_specs=[VMEM] * 9,
        out_specs=(VMEM, VMEM),
        name="edge_offsets",
    )(source, elem_type, lat_velocity, inlet_trace, inner, couple, own, from_left, from_right)
    if not packed:
        part = columns // flow_n
        send = send.reshape(species, trace + levels, flow_n, part)
        send = send.transpose(2, 1, 0, 3).reshape(flow_n, trace + levels, species * part)
    got = lax.all_to_all(send, "flow", 0, 0, tiled=True)

    top_table = solve_table[:, :, dofs - trace :, dofs:]
    back = pl.pallas_call(
        owner_kernel,
        out_shape=shape((flow_n, trace, got.shape[2]), F32),
        in_specs=[VMEM, VMEM],
        out_specs=VMEM,
        scratch_shapes=[pltpu.VMEM((types_n, trace, trace, got.shape[2]), F32)],
        name="owner_sweep",
    )(top_table, got)
    traces = lax.all_to_all(back, "flow", 0, 0, tiled=True)
    if not packed:
        traces = traces.reshape(flow_n, trace, species, part)
        traces = traces.transpose(2, 1, 0, 3).reshape(species, trace, columns)

    return pl.pallas_call(
        final_kernel,
        out_shape=shape((species, levels, dofs, columns), BF16),
        in_specs=[VMEM] * 6,
        out_specs=ANY,
        scratch_shapes=[
            pltpu.VMEM((species, levels, dofs, columns), BF16),
            pltpu.SemaphoreType.DMA((pairs,)),
        ],
        name="final_sweep",
    )(source, elem_type, inlet_trace, couple, corr, traces)


def solution(mesh):
    in_specs = (
        P(None, "flow", None, "lat"),
        P("flow", "lat"),
        P("flow", "lat"),
        P(None, None, "lat"),
        P(),
    )
    out_specs = P(None, "flow", None, "lat")
    return jax.shard_map(
        on_device, mesh=mesh, in_specs=in_specs, out_specs=out_specs, check_vma=False
    )
```

```python
import jax
import jax.numpy as jnp
from jax import lax
from jax.experimental import pallas as pl
from jax.experimental.pallas import tpu as pltpu
from jax.sharding import PartitionSpec as P

F32 = jnp.float32
BF16 = jnp.bfloat16
VMEM = pl.BlockSpec(memory_space=pltpu.VMEM)
ANY = pl.BlockSpec(memory_space=pl.ANY)
LANES = 128
PARAMS = pltpu.CompilerParams(vmem_limit_bytes=20 << 20)


def lane_index(shape):
    return lax.broadcasted_iota(jnp.int32, shape, len(shape) - 1)


def split(x):
    hi = x.astype(BF16)
    return hi, (x - hi.astype(F32)).astype(BF16)


def stacked_parts(x):
    hi, lo = split(x)
    return jnp.concatenate([hi, lo, hi], axis=0)


def pick(per_type, types, rows):
    columns = per_type.shape[1]
    grid = per_type.reshape(-1, rows // 8, 8, columns)
    out = grid[0]
    for t in range(1, grid.shape[0]):
        out = jnp.where((types == t)[None], grid[t], out)
    return out.reshape(rows, columns)


def masked_parts(x, onehot_ref, level):
    hi, lo = split(x)
    parts = []
    for t in range(onehot_ref.shape[1]):
        mask = onehot_ref[level, t]
        his = hi * mask
        parts += [his, lo * mask, his]
    return jnp.concatenate(parts, axis=0)


def mm(a, b):
    return jnp.dot(a, b, preferred_element_type=F32)


def load_kernel(conc_hbm, vel_ref, x_ref, right_ref, left_ref, sems):
    species, tiles, levels, dofs, _ = x_ref.shape
    trace = right_ref.shape[0]
    stride = dofs // trace
    copies = []
    for k in [0, tiles - 1, *range(1, tiles - 1)]:
        for s in range(species):
            block = conc_hbm.at[s, :, :, pl.ds(k * LANES, LANES)]
            copies.append(pltpu.make_async_copy(block, x_ref.at[s, k], sems.at[s * tiles + k]))
            copies[-1].start()
    lane = lane_index((levels, LANES))
    on_diag = lane % levels == lax.broadcasted_iota(jnp.int32, lane.shape, 0)
    face = jnp.broadcast_to(vel_ref[:, :1], (levels, LANES))
    face = jnp.sum(jnp.where(on_diag, face, 0.0), axis=0, keepdims=True)
    left_ref[trace:] = jnp.broadcast_to(face, (left_ref.shape[0] - trace, LANES))
    for copy in copies[: 2 * species]:
        copy.wait()
    lane = lane_index((trace, LANES))
    right = jnp.zeros((trace, LANES), F32)
    left = jnp.zeros((trace, LANES), F32)
    for p in range(species * levels):
        s, l = p // levels, p % levels
        last = x_ref[s, tiles - 1, l, pl.ds(stride - 1, trace, stride=stride), :]
        first = x_ref[s, 0, l, pl.ds(0, trace, stride=stride), :]
        right = jnp.where(lane == p, pltpu.roll(last, (p + 1) % LANES, 1), right)
        left = jnp.where(lane == p, pltpu.roll(first, p, 1) if p else first, left)
    right_ref[...] = right
    left_ref[:trace] = left
    for copy in copies[2 * species :]:
        copy.wait()


def inner_kernel(
    x_ref, vel_ref, type_ref, table_ref, mid_ref, rim_ref, top_ref, a_top_ref, a_rest_ref, c_ref, onehot_ref,
    delta_ref,
):
    species, tiles_n, levels, dofs, _ = x_ref.shape
    columns = tiles_n * LANES
    types_n, trace = onehot_ref.shape[1], onehot_ref.shape[2]
    stride = dofs // trace
    rest = dofs - trace
    for s in range(species):
        tops, rests = [], []
        pieces = [[], [], []]
        for t in range(types_n):
            table = table_ref[s, t]
            hi = table.astype(BF16).astype(F32)
            lo = table - hi
            lane = lane_index(table.shape)
            twice = jnp.where(lane < dofs, hi, pltpu.roll(hi, dofs, 1))
            wide = jnp.concatenate([twice, lo[:, :dofs]], axis=1).astype(BF16)
            tops.append(wide[rest:])
            rests.append(wide[:rest])
            pieces[0].append(hi)
            pieces[2].append(lo)
        a_top_ref[s] = jnp.concatenate(tops, axis=0)
        a_rest_ref[s] = jnp.concatenate(rests, axis=0)
        pieces[1] = pieces[0]
        count = 3 * types_n * trace
        tiles = []
        for start in range(0, count, LANES):
            lane = lane_index((dofs, LANES))
            tile = jnp.zeros((dofs, LANES), F32)
            for at in range(start, min(count, start + LANES), trace):
                k = at // trace
                piece = pltpu.roll(pieces[k % 3][k // 3], (at - start - dofs) % LANES, 1)
                inside = (lane >= at - start) & (lane < at - start + trace)
                tile = jnp.where(inside, piece, tile)
            tiles.append(jnp.concatenate([tile[rest:], tile[:rest]], axis=0).astype(BF16))
        c_ref[s] = jnp.concatenate(tiles, axis=1)[:, :count]
    for k in range(delta_ref.shape[0]):
        delta_ref[k] = jnp.zeros((tiles_n, dofs, LANES), F32)
    lane = lane_index((trace, columns))
    for l in range(levels):
        velocity = jnp.broadcast_to(vel_ref[l : l + 1], (trace, columns))
        plus = jnp.where(lane > 0, jnp.maximum(velocity, 0.0), 0.0)
        minus = jnp.minimum(velocity, 0.0)
        types = jnp.broadcast_to(type_ref[l : l + 1], (trace, columns))
        for t in range(types_n):
            onehot_ref[l, t] = jnp.where(types == t, 1.0, 0.0).astype(BF16)
        types_mid = types[:8, LANES : columns - LANES]
        for s in range(species):
            k = (l * species + s) % delta_ref.shape[0]
            zero, three = pl.ds(0, trace, stride=stride), pl.ds(stride - 1, trace, stride=stride)
            low = jnp.concatenate([x_ref[s, i, l, zero, :] for i in range(tiles_n)], axis=1)
            high = jnp.concatenate([x_ref[s, i, l, three, :] for i in range(tiles_n)], axis=1)
            flux = plus * pltpu.roll(high, 1, 1) + minus * low
            out = jnp.where(lane == columns - 1, 0.0, -pltpu.roll(flux, columns - 1, 1))
            source = []
            for i in range(tiles_n):
                delta_ref[k, i, zero, :] = flux[:, i * LANES : (i + 1) * LANES]
                delta_ref[k, i, three, :] = out[:, i * LANES : (i + 1) * LANES]
                source.append(x_ref[s, i, l] + delta_ref[k, i])
            mid = jnp.concatenate(source[1:-1], axis=1)
            mid_ref[s, l] = mid
            rim_ref[s, l, 0] = source[0]
            rim_ref[s, l, 1] = source[-1]
            top_ref[s, l] = pick(mm(a_top_ref[s], stacked_parts(mid)), types_mid, trace)


def offset_kernel(
    rim_ref, mid_top_ref, type_ref, onehot_ref, inlet_ref, a_top_ref, c_ref, own_right_ref, own_left_ref, from_left_ref,
    from_right_ref, edge_ref, top_ref, send_ref,
):
    species, levels, trace, columns = top_ref.shape
    dofs = rim_ref.shape[3]
    stride = dofs // trace
    lat, lat_n = lax.axis_index("lat"), lax.axis_size("lat")
    has_left = (lat > 0).astype(F32)
    has_right = (lat < lat_n - 1).astype(F32)

    def face(ref):
        return jnp.broadcast_to(ref[trace : trace + 1], (trace, LANES))

    coming = jnp.maximum(face(own_left_ref), 0.0) * from_left_ref[...] * has_left
    velocity = face(from_right_ref)
    leaving = jnp.maximum(velocity, 0.0) * own_right_ref[...]
    leaving = (leaving + jnp.minimum(velocity, 0.0) * from_right_ref[:trace]) * has_right
    lane = lane_index((trace, LANES))
    for l in range(levels):
        for s in range(species):
            p = s * levels + l
            first = jnp.where(lane == 0, pltpu.roll(coming, (LANES - p) % LANES, 1), 0.0)
            last = jnp.where(lane == LANES - 1, pltpu.roll(leaving, LANES - 1 - p, 1), 0.0)
            low, high = pl.ds(0, trace, stride=stride), pl.ds(stride - 1, trace, stride=stride)
            edge_ref[s, l] = rim_ref[s, l]
            edge_ref[s, l, 0, low, :] = rim_ref[s, l, 0, low, :] + first
            edge_ref[s, l, 1, high, :] = rim_ref[s, l, 1, high, :] - last
    for l in range(levels):
        types = jnp.broadcast_to(type_ref[l : l + 1], (8, columns))
        rim_types = jnp.concatenate([types[:, :LANES], types[:, columns - LANES :]], axis=1)
        for s in range(species):
            source = jnp.concatenate([edge_ref[s, l, 0], edge_ref[s, l, 1]], axis=1)
            top = pick(mm(a_top_ref[s], stacked_parts(source)), rim_types, trace)
            top_ref[s, l] = jnp.concatenate([top[:, :LANES], mid_top_ref[s, l], top[:, LANES:]], axis=1)
    start = (lax.axis_index("flow") == 0).astype(F32)
    traces = [inlet_ref[s] * start for s in range(species)]
    for l in range(levels):
        for s in range(species):
            moved = mm(c_ref[s, :trace], masked_parts(traces[s], onehot_ref, l))
            traces[s] = moved + top_ref[s, l]
    width = send_ref.shape[2]
    types = type_ref[...].astype(F32)
    if width == LANES:
        half = width // 2
        low = lane_index((trace, width)) < half
        low_t = lane_index((levels, width)) < half
        for k in range(columns // width):
            a, b = (traces[s][:, k * width : (k + 1) * width] for s in (0, 1))
            t = types[:, k * width : (k + 1) * width]
            swapped = pltpu.roll(t, half, 1)
            send_ref[2 * k, :trace] = jnp.where(low, a, pltpu.roll(b, half, 1))
            send_ref[2 * k + 1, :trace] = jnp.where(low, pltpu.roll(a, half, 1), b)
            send_ref[2 * k, trace:] = jnp.where(low_t, t, swapped)
            send_ref[2 * k + 1, trace:] = jnp.where(low_t, swapped, t)
    else:
        for s in range(species):
            send_ref[s, :trace] = traces[s]
            send_ref[s, trace:] = types


def rest_kernel(mid_ref, edge_ref, type_ref, a_rest_ref, table_ref, rest_ref, coef_ref):
    species, levels, rest, columns = rest_ref.shape
    types_n, trace, width = coef_ref.shape[0], coef_ref.shape[1], coef_ref.shape[3]
    dofs = rest + trace
    half = width // species
    which = lane_index((trace, width)) // half
    for t in range(types_n):
        for j in range(trace):
            column = slice(dofs + j, dofs + j + 1)
            value = jnp.broadcast_to(table_ref[0, t, rest:, column], (trace, width))
            for s in range(1, species):
                other = jnp.broadcast_to(table_ref[s, t, rest:, column], (trace, width))
                value = jnp.where(which == s, other, value)
            coef_ref[t, j] = value
    for l in range(levels):
        types = jnp.broadcast_to(type_ref[l : l + 1], (8, columns))
        for s in range(species):
            source = jnp.concatenate([edge_ref[s, l, 0], mid_ref[s, l], edge_ref[s, l, 1]], axis=1)
            rest_ref[s, l] = pick(mm(a_rest_ref[s], stacked_parts(source)), types, rest)


def owner_kernel(coef_ref, got_ref, out_ref):
    slabs, _, width = got_ref.shape
    types_n, trace = coef_ref.shape[:2]
    levels = got_ref.shape[1] - trace
    out_ref[0] = jnp.zeros((trace, width), F32)

    def slab(g, state):
        out_ref[g] = state
        for l in range(levels):
            types = jnp.broadcast_to(got_ref[g, trace + l : trace + l + 1], (trace, width))
            chosen = [types == float(t) for t in range(1, types_n)]
            terms = []
            for j in range(trace):
                coef = coef_ref[0, j]
                for t in range(1, types_n):
                    coef = jnp.where(chosen[t - 1], coef_ref[t, j], coef)
                terms.append(coef * state[j : j + 1])
            while len(terms) > 1:
                terms = [a + b for a, b in zip(terms[::2], terms[1::2])]
            state = terms[0]
        return state + got_ref[g, :trace]

    last = lax.fori_loop(1, slabs - 1, slab, got_ref[0, :trace])
    out_ref[slabs - 1] = last


def final_kernel(top_ref, rest_ref, onehot_ref, inlet_ref, c_ref, got_ref, out_hbm, o_ref, sems):
    species, levels, trace, columns = top_ref.shape
    rest = rest_ref.shape[2]
    width = got_ref.shape[2]
    is_first = lax.axis_index("flow") == 0
    if width == LANES:
        half = width // 2
        low = lane_index((trace, width)) < half
        tiles = [[], []]
        for k in range(columns // width):
            a, b = got_ref[2 * k], got_ref[2 * k + 1]
            tiles[0].append(jnp.where(low, a, pltpu.roll(b, half, 1)))
            tiles[1].append(jnp.where(low, pltpu.roll(a, half, 1), b))
        received = [jnp.concatenate(t, axis=1) for t in tiles]
    else:
        received = [got_ref[s] for s in range(species)]
    traces = [jnp.where(is_first, inlet_ref[s], received[s]) for s in range(species)]
    copies = []
    for l in range(levels):
        for s in range(species):
            moved = mm(c_ref[s], masked_parts(traces[s], onehot_ref, l))
            traces[s] = moved[:trace] + top_ref[s, l]
            o_ref[s, l, rest:] = traces[s].astype(BF16)
            o_ref[s, l, :rest] = (moved[trace:] + rest_ref[s, l]).astype(BF16)
            copies.append(
                pltpu.make_async_copy(o_ref.at[s, l], out_hbm.at[s, l], sems.at[s * levels + l])
            )
            copies[-1].start()
    for copy in copies:
        copy.wait()


def on_device(conc_old, lat_velocity, elem_type, inlet_trace, solve_table):
    species, levels, dofs, columns = conc_old.shape
    types_n = solve_table.shape[1]
    trace = inlet_trace.shape[1]
    flow_n = lax.axis_size("flow")
    lat_n = lax.axis_size("lat")
    pairs = species * levels
    tiles = columns // LANES
    inner = columns - 2 * LANES
    rest = dofs - trace

    def shape(dims, kind=F32):
        return jax.ShapeDtypeStruct(dims, kind)

    def cost(rows, count):
        flops = 2 * 3 * types_n * rows * dofs * count * pairs
        return pl.CostEstimate(
            flops=flops, bytes_accessed=8 * pairs * dofs * columns, transcendentals=0
        )

    x, right, left = pl.pallas_call(
        load_kernel,
        out_shape=(shape((species, tiles, levels, dofs, LANES)), shape((trace, LANES)), shape((trace + 8, LANES))),
        in_specs=[ANY, VMEM],
        out_specs=(VMEM, VMEM, VMEM),
        scratch_shapes=[pltpu.SemaphoreType.DMA((species * tiles,))],
        compiler_params=PARAMS,
        name="load_edges",
    )(conc_old, lat_velocity)
    from_left = lax.ppermute(right, "lat", [(i, (i + 1) % lat_n) for i in range(lat_n)])
    from_right = lax.ppermute(left, "lat", [((i + 1) % lat_n, i) for i in range(lat_n)])


    table = jnp.pad(solve_table, ((0, 0), (0, 0), (0, 0), (0, LANES - dofs - trace)))
    mid, rim, mid_top, a_top, a_rest, c_all, onehot = pl.pallas_call(
        inner_kernel,
        out_shape=(
            shape((species, levels, dofs, inner)),
            shape((species, levels, 2, dofs, LANES)),
            shape((species, levels, trace, inner)),
            shape((species, types_n * trace, 3 * dofs), BF16),
            shape((species, types_n * rest, 3 * dofs), BF16),
            shape((species, dofs, 3 * types_n * trace), BF16),
            shape((levels, types_n, trace, columns), BF16),
        ),
        in_specs=[VMEM] * 4,
        out_specs=(VMEM,) * 7,
        scratch_shapes=[pltpu.VMEM((4, tiles, dofs, LANES), F32)],
        compiler_params=PARAMS,
        cost_estimate=cost(dofs, columns),
        name="inner_sources",
    )(x, lat_velocity, elem_type, table)

    packed = 2 * columns == LANES * flow_n and species == 2
    send_shape = (flow_n, trace + levels, LANES) if packed else (species, trace + levels, columns)
    edge, top, send = pl.pallas_call(
        offset_kernel,
        out_shape=(
            shape((species, levels, 2, dofs, LANES)),
            shape((species, levels, trace, columns)),
            shape(send_shape),
        ),
        in_specs=[VMEM] * 11,
        out_specs=(VMEM, VMEM, VMEM),
        compiler_params=PARAMS,
        name="slab_offsets",
    )(
        rim, mid_top, elem_type, onehot, inlet_trace, a_top, c_all, right, left, from_left, from_right
    )
    part = columns // flow_n
    if not packed:
        send = send.reshape(species, trace + levels, flow_n, part)
        send = send.transpose(2, 1, 0, 3).reshape(flow_n, trace + levels, species * part)
    got = lax.all_to_all(send, "flow", 0, 0, tiled=True)

    rest_terms, coef = pl.pallas_call(
        rest_kernel,
        out_shape=(
            shape((species, levels, rest, columns)),
            shape((types_n, trace, trace, species * part)),
        ),
        in_specs=[VMEM] * 5,
        out_specs=(VMEM, VMEM),
        compiler_params=PARAMS,
        cost_estimate=cost(rest, columns),
        name="rest_sources",
    )(mid, edge, elem_type, a_rest, table)
    back = pl.pallas_call(
        owner_kernel,
        out_shape=shape((flow_n, trace, species * part)),
        in_specs=[VMEM, VMEM],
        out_specs=VMEM,
        compiler_params=PARAMS,
        name="owner_sweep",
    )(coef, got)
    traces = lax.all_to_all(back, "flow", 0, 0, tiled=True)
    if not packed:
        traces = traces.reshape(flow_n, trace, species, part)
        traces = traces.transpose(2, 1, 0, 3).reshape(species, trace, columns)

    return pl.pallas_call(
        final_kernel,
        out_shape=shape(conc_old.shape, BF16),
        in_specs=[VMEM] * 6,
        out_specs=ANY,
        scratch_shapes=[
            pltpu.VMEM(conc_old.shape, BF16),
            pltpu.SemaphoreType.DMA((pairs,)),
        ],
        compiler_params=PARAMS,
        name="final_sweep",
    )(top, rest_terms, onehot, inlet_trace, c_all, traces)


def solution(mesh):
    in_specs = (
        P(None, "flow", None, "lat"),
        P("flow", "lat"),
        P("flow", "lat"),
        P(None, None, "lat"),
        P(),
    )
    out_specs = P(None, "flow", None, "lat")
    return jax.shard_map(
        on_device, mesh=mesh, in_specs=in_specs, out_specs=out_specs, check_vma=False
    )
```

```python
import jax
import jax.numpy as jnp
from jax import lax
from jax.experimental import pallas as pl
from jax.experimental.pallas import tpu as pltpu
from jax.sharding import PartitionSpec as P

F32 = jnp.float32
BF16 = jnp.bfloat16
VMEM = pl.BlockSpec(memory_space=pltpu.VMEM)
HBM = pl.BlockSpec(memory_space=pltpu.HBM)
LANES = 128
PARAMS = pltpu.CompilerParams(vmem_limit_bytes=20 << 20)


def lane_index(shape):
    return lax.broadcasted_iota(jnp.int32, shape, len(shape) - 1)


def split(x):
    hi = x.astype(BF16)
    return hi, (x - hi.astype(F32)).astype(BF16)


def stacked_parts(x):
    hi, lo = split(x)
    return jnp.concatenate([hi, lo, hi], axis=0)


def pick(per_type, types, rows):
    columns = per_type.shape[1]
    grid = per_type.reshape(-1, rows // 8, 8, columns)
    out = grid[0]
    for t in range(1, grid.shape[0]):
        out = jnp.where((types == t)[None], grid[t], out)
    return out.reshape(rows, columns)


def masked_parts(x, masks):
    hi, lo = split(x)
    parts = []
    for mask in masks:
        his = hi * mask
        parts += [his, lo * mask, his]
    return jnp.concatenate(parts, axis=0)


def masks_of(type_ref, level, types_n, rows):
    types = jnp.broadcast_to(type_ref[level : level + 1], (rows, type_ref.shape[1]))
    return [jnp.where(types == t, 1.0, 0.0).astype(BF16) for t in range(types_n)]


def mm(a, b):
    return jnp.dot(a, b, preferred_element_type=F32)


def load_kernel(
    conc_hbm, vel_hbm, type_hbm, table_hbm, inlet_hbm, x_ref, vel_ref, type_ref, table_ref, inlet_ref, right_ref, left_ref,
    sems, small_sems,
):
    species, tiles, levels, dofs, _ = x_ref.shape
    trace = right_ref.shape[0]
    stride = dofs // trace
    copies = []
    for k in [0, tiles - 1, *range(1, tiles - 1)]:
        for s in range(species):
            block = conc_hbm.at[s, :, :, pl.ds(k * LANES, LANES)]
            copies.append(pltpu.make_async_copy(block, x_ref.at[s, k], sems.at[s * tiles + k]))
            copies[-1].start()
        if k == tiles - 1:
            small = ((vel_hbm, vel_ref), (type_hbm, type_ref), (table_hbm, table_ref), (inlet_hbm, inlet_ref))
            small = [pltpu.make_async_copy(*ends, small_sems.at[i]) for i, ends in enumerate(small)]
            for copy in small:
                copy.start()
    small[0].wait()
    lane = lane_index((levels, LANES))
    on_diag = lane % levels == lax.broadcasted_iota(jnp.int32, lane.shape, 0)
    face = jnp.broadcast_to(vel_ref[:, :1], (levels, LANES))
    face = jnp.sum(jnp.where(on_diag, face, 0.0), axis=0, keepdims=True)
    left_ref[trace:] = jnp.broadcast_to(face, (left_ref.shape[0] - trace, LANES))
    for copy in copies[: 2 * species]:
        copy.wait()
    lane = lane_index((trace, LANES))
    right = jnp.zeros((trace, LANES), F32)
    left = jnp.zeros((trace, LANES), F32)
    for p in range(species * levels):
        s, l = p // levels, p % levels
        last = x_ref[s, tiles - 1, l, pl.ds(stride - 1, trace, stride=stride), :]
        first = x_ref[s, 0, l, pl.ds(0, trace, stride=stride), :]
        right = jnp.where(lane == p, pltpu.roll(last, (p + 1) % LANES, 1), right)
        left = jnp.where(lane == p, pltpu.roll(first, p, 1) if p else first, left)
    right_ref[...] = right
    left_ref[:trace] = left
    for copy in copies[2 * species :] + small[1:]:
        copy.wait()


def inner_kernel(
    x_ref, vel_ref, type_ref, table_ref, rest_ref, rim_ref, top_ref, a_top_ref, a_rest_ref, c_ref, small_ref, delta_ref
):
    species, tiles_n, levels, dofs, _ = x_ref.shape
    columns = tiles_n * LANES
    types_n, trace = small_ref.shape[1], small_ref.shape[2]
    stride = dofs // trace
    rest = dofs - trace
    for s in range(species):
        tops, rests = [], []
        pieces = [[], [], []]
        for t in range(types_n):
            table = table_ref[s, t]
            table = jnp.concatenate([table, jnp.zeros((dofs, LANES - table.shape[1]), F32)], axis=1)
            hi = table.astype(BF16).astype(F32)
            lo = table - hi
            lane = lane_index(table.shape)
            twice = jnp.where(lane < dofs, hi, pltpu.roll(hi, dofs, 1))
            wide = jnp.concatenate([twice, lo[:, :dofs]], axis=1).astype(BF16)
            small_ref[s, t] = table_ref[s, t, rest:, dofs:]
            tops.append(wide[rest:])
            rests.append(wide[:rest])
            pieces[0].append(hi)
            pieces[2].append(lo)
        a_top_ref[s] = jnp.concatenate(tops, axis=0)
        a_rest_ref[s] = jnp.concatenate(rests, axis=0)
        pieces[1] = pieces[0]
        count = 3 * types_n * trace
        tiles = []
        for start in range(0, count, LANES):
            lane = lane_index((dofs, LANES))
            tile = jnp.zeros((dofs, LANES), F32)
            for at in range(start, min(count, start + LANES), trace):
                k = at // trace
                piece = pltpu.roll(pieces[k % 3][k // 3], (at - start - dofs) % LANES, 1)
                inside = (lane >= at - start) & (lane < at - start + trace)
                tile = jnp.where(inside, piece, tile)
            tiles.append(jnp.concatenate([tile[rest:], tile[:rest]], axis=0).astype(BF16))
        c_ref[s] = jnp.concatenate(tiles, axis=1)[:, :count]
    for k in range(delta_ref.shape[0]):
        delta_ref[k] = jnp.zeros((tiles_n, dofs, LANES), F32)
    lane = lane_index((trace, columns))
    for l in range(levels):
        velocity = jnp.broadcast_to(vel_ref[l : l + 1], (trace, columns))
        plus = jnp.where(lane > 0, jnp.maximum(velocity, 0.0), 0.0)
        minus = jnp.minimum(velocity, 0.0)
        types = jnp.broadcast_to(type_ref[l : l + 1], (8, columns))[:, LANES : columns - LANES]
        for s in range(species):
            k = (l * species + s) % delta_ref.shape[0]
            zero, three = pl.ds(0, trace, stride=stride), pl.ds(stride - 1, trace, stride=stride)
            low = jnp.concatenate([x_ref[s, i, l, zero, :] for i in range(tiles_n)], axis=1)
            high = jnp.concatenate([x_ref[s, i, l, three, :] for i in range(tiles_n)], axis=1)
            flux = plus * pltpu.roll(high, 1, 1) + minus * low
            out = jnp.where(lane == columns - 1, 0.0, -pltpu.roll(flux, columns - 1, 1))
            source = []
            for i in range(tiles_n):
                delta_ref[k, i, zero, :] = flux[:, i * LANES : (i + 1) * LANES]
                delta_ref[k, i, three, :] = out[:, i * LANES : (i + 1) * LANES]
                source.append(x_ref[s, i, l] + delta_ref[k, i])
            parts = stacked_parts(jnp.concatenate(source[1:-1], axis=1))
            rim_ref[s, l, 0] = source[0]
            rim_ref[s, l, 1] = source[-1]
            top_ref[s, l] = pick(mm(a_top_ref[s], parts), types, trace)
            rest_ref[s, l] = pick(mm(a_rest_ref[s], parts), types, rest)


def offset_kernel(
    rim_ref, mid_top_ref, type_ref, inlet_ref, a_top_ref, c_ref, own_right_ref, own_left_ref, from_left_ref, from_right_ref,
    edge_hbm, top_ref, send_ref, edge_ref, sems,
):
    species, levels, trace, columns = top_ref.shape
    dofs = rim_ref.shape[3]
    stride = dofs // trace
    lat, lat_n = lax.axis_index("lat"), lax.axis_size("lat")
    has_left = (lat > 0).astype(F32)
    has_right = (lat < lat_n - 1).astype(F32)

    def face(ref):
        return jnp.broadcast_to(ref[trace : trace + 1], (trace, LANES))

    coming = jnp.maximum(face(own_left_ref), 0.0) * from_left_ref[...] * has_left
    velocity = face(from_right_ref)
    leaving = jnp.maximum(velocity, 0.0) * own_right_ref[...]
    leaving = (leaving + jnp.minimum(velocity, 0.0) * from_right_ref[:trace]) * has_right
    lane = lane_index((trace, LANES))
    for l in range(levels):
        for s in range(species):
            p = s * levels + l
            first = jnp.where(lane == 0, pltpu.roll(coming, (LANES - p) % LANES, 1), 0.0)
            last = jnp.where(lane == LANES - 1, pltpu.roll(leaving, LANES - 1 - p, 1), 0.0)
            low, high = pl.ds(0, trace, stride=stride), pl.ds(stride - 1, trace, stride=stride)
            edge_ref[s, l] = rim_ref[s, l]
            edge_ref[s, l, 0, low, :] = rim_ref[s, l, 0, low, :] + first
            edge_ref[s, l, 1, high, :] = rim_ref[s, l, 1, high, :] - last
    copies = [pltpu.make_async_copy(edge_ref.at[s], edge_hbm.at[s], sems.at[s]) for s in range(species)]
    for copy in copies:
        copy.start()
    for l in range(levels):
        types = jnp.broadcast_to(type_ref[l : l + 1], (8, columns))
        rim_types = jnp.concatenate([types[:, :LANES], types[:, columns - LANES :]], axis=1)
        for s in range(species):
            source = jnp.concatenate([edge_ref[s, l, 0], edge_ref[s, l, 1]], axis=1)
            top = pick(mm(a_top_ref[s], stacked_parts(source)), rim_types, trace)
            top_ref[s, l] = jnp.concatenate([top[:, :LANES], mid_top_ref[s, l], top[:, LANES:]], axis=1)
    start = (lax.axis_index("flow") == 0).astype(F32)
    traces = [inlet_ref[s] * start for s in range(species)]
    for l in range(levels):
        masks = masks_of(type_ref, l, a_top_ref.shape[1] // trace, trace)
        for s in range(species):
            moved = mm(c_ref[s, :trace], masked_parts(traces[s], masks))
            traces[s] = moved + top_ref[s, l]
    width = send_ref.shape[2]
    types = type_ref[...].astype(F32)
    if width == LANES:
        half = width // 2
        low = lane_index((trace, width)) < half
        low_t = lane_index((levels, width)) < half
        for k in range(columns // width):
            a, b = (traces[s][:, k * width : (k + 1) * width] for s in (0, 1))
            t = types[:, k * width : (k + 1) * width]
            swapped = pltpu.roll(t, half, 1)
            send_ref[2 * k, :trace] = jnp.where(low, a, pltpu.roll(b, half, 1))
            send_ref[2 * k + 1, :trace] = jnp.where(low, pltpu.roll(a, half, 1), b)
            send_ref[2 * k, trace:] = jnp.where(low_t, t, swapped)
            send_ref[2 * k + 1, trace:] = jnp.where(low_t, swapped, t)
    else:
        for s in range(species):
            send_ref[s, :trace] = traces[s]
            send_ref[s, trace:] = types
    for copy in copies:
        copy.wait()


def rest_kernel(edge_hbm, type_ref, a_rest_ref, small_ref, rest_ref, coef_ref, edge_ref, sems):
    species, levels, rest, _ = rest_ref.shape
    columns = type_ref.shape[1]
    types_n, trace, width = coef_ref.shape[0], coef_ref.shape[1], coef_ref.shape[3]
    copies = [pltpu.make_async_copy(edge_hbm.at[s], edge_ref.at[s], sems.at[s]) for s in range(species)]
    for copy in copies:
        copy.start()
    half = width // species
    which = lane_index((trace, width)) // half
    for t in range(types_n):
        for j in range(trace):
            value = jnp.broadcast_to(small_ref[0, t, :, j : j + 1], (trace, width))
            for s in range(1, species):
                other = jnp.broadcast_to(small_ref[s, t, :, j : j + 1], (trace, width))
                value = jnp.where(which == s, other, value)
            coef_ref[t, j] = value
    for copy in copies:
        copy.wait()
    for l in range(levels):
        types = jnp.broadcast_to(type_ref[l : l + 1], (8, columns))
        types = jnp.concatenate([types[:, :LANES], types[:, columns - LANES :]], axis=1)
        for s in range(species):
            source = jnp.concatenate([edge_ref[s, l, 0], edge_ref[s, l, 1]], axis=1)
            rest_ref[s, l] = pick(mm(a_rest_ref[s], stacked_parts(source)), types, rest)


def owner_kernel(coef_ref, got_ref, out_ref):
    slabs, _, width = got_ref.shape
    types_n, trace = coef_ref.shape[:2]
    levels = got_ref.shape[1] - trace
    out_ref[0] = jnp.zeros((trace, width), F32)

    def slab(g, state):
        out_ref[g] = state
        for l in range(levels):
            types = jnp.broadcast_to(got_ref[g, trace + l : trace + l + 1], (trace, width))
            chosen = [types == float(t) for t in range(1, types_n)]
            terms = []
            for j in range(trace):
                coef = coef_ref[0, j]
                for t in range(1, types_n):
                    coef = jnp.where(chosen[t - 1], coef_ref[t, j], coef)
                terms.append(coef * state[j : j + 1])
            while len(terms) > 1:
                terms = [a + b for a, b in zip(terms[::2], terms[1::2])]
            state = terms[0]
        return state + got_ref[g, :trace]

    last = lax.fori_loop(1, slabs - 1, slab, got_ref[0, :trace])
    out_ref[slabs - 1] = last


def final_kernel(
    top_ref, inner_rest_ref, outer_rest_ref, type_ref, inlet_ref, c_ref, got_ref, out_hbm, o_ref, sems
):
    species, levels, trace, columns = top_ref.shape
    rest = inner_rest_ref.shape[2]
    types_n = c_ref.shape[2] // (3 * trace)
    width = got_ref.shape[2]
    is_first = lax.axis_index("flow") == 0
    if width == LANES:
        half = width // 2
        low = lane_index((trace, width)) < half
        tiles = [[], []]
        for k in range(columns // width):
            a, b = got_ref[2 * k], got_ref[2 * k + 1]
            tiles[0].append(jnp.where(low, a, pltpu.roll(b, half, 1)))
            tiles[1].append(jnp.where(low, pltpu.roll(a, half, 1), b))
        received = [jnp.concatenate(t, axis=1) for t in tiles]
    else:
        received = [got_ref[s] for s in range(species)]
    traces = [jnp.where(is_first, inlet_ref[s], received[s]) for s in range(species)]
    copies = []
    for l in range(levels):
        masks = masks_of(type_ref, l, types_n, trace)
        for s in range(species):
            moved = mm(c_ref[s], masked_parts(traces[s], masks))
            traces[s] = moved[:trace] + top_ref[s, l]
            o_ref[s, l, rest:] = traces[s].astype(BF16)
            outer = outer_rest_ref[s, l]
            fixed = jnp.concatenate([outer[:, :LANES], inner_rest_ref[s, l], outer[:, LANES:]], axis=1)
            o_ref[s, l, :rest] = (moved[trace:] + fixed).astype(BF16)
            copies.append(
                pltpu.make_async_copy(o_ref.at[s, l], out_hbm.at[s, l], sems.at[s * levels + l])
            )
            copies[-1].start()
    for copy in copies:
        copy.wait()


def on_device(conc_old, lat_velocity, elem_type, inlet_trace, solve_table):
    species, levels, dofs, columns = conc_old.shape
    types_n = solve_table.shape[1]
    trace = inlet_trace.shape[1]
    flow_n = lax.axis_size("flow")
    lat_n = lax.axis_size("lat")
    pairs = species * levels
    tiles = columns // LANES
    inner = columns - 2 * LANES
    rest = dofs - trace

    def shape(dims, kind=F32):
        return jax.ShapeDtypeStruct(dims, kind)

    def held(dims, kind=F32):
        return pltpu.VMEM(dims, kind)

    def far(array):
        return pltpu.with_memory_space_constraint(array, pltpu.HBM)

    def cost(rows, count):
        flops = 2 * 3 * types_n * rows * dofs * count * pairs
        return pl.CostEstimate(
            flops=flops, bytes_accessed=8 * pairs * dofs * columns, transcendentals=0
        )

    x, velocity, types, table, inlet, right, left = pl.pallas_call(
        load_kernel,
        out_shape=(
            held((species, tiles, levels, dofs, LANES)),
            held(lat_velocity.shape),
            held(elem_type.shape, elem_type.dtype),
            held(solve_table.shape),
            held(inlet_trace.shape),
            shape((trace, LANES)),
            shape((trace + 8, LANES)),
        ),
        in_specs=[HBM] * 5,
        out_specs=(VMEM,) * 7,
        scratch_shapes=[pltpu.SemaphoreType.DMA((species * tiles,)), pltpu.SemaphoreType.DMA((4,))],
        compiler_params=PARAMS,
        name="load_edges",
    )(far(conc_old), far(lat_velocity), far(elem_type), far(solve_table), far(inlet_trace))
    from_left = lax.ppermute(right, "lat", [(i, (i + 1) % lat_n) for i in range(lat_n)])
    from_right = lax.ppermute(left, "lat", [((i + 1) % lat_n, i) for i in range(lat_n)])


    inner_rest, rim, mid_top, a_top, a_rest, c_all, small = pl.pallas_call(
        inner_kernel,
        out_shape=(
            held((species, levels, rest, inner)),
            held((species, levels, 2, dofs, LANES)),
            held((species, levels, trace, inner)),
            held((species, types_n * trace, 3 * dofs), BF16),
            held((species, types_n * rest, 3 * dofs), BF16),
            held((species, dofs, 3 * types_n * trace), BF16),
            held((species, types_n, trace, trace)),
        ),
        in_specs=[VMEM] * 4,
        out_specs=(VMEM,) * 7,
        scratch_shapes=[pltpu.VMEM((4, tiles, dofs, LANES), F32)],
        compiler_params=PARAMS,
        cost_estimate=cost(dofs, columns),
        name="inner_sources",
    )(x, velocity, types, table)

    edge_shape = (species, levels, 2, dofs, LANES)
    packed = 2 * columns == LANES * flow_n and species == 2
    send_shape = (flow_n, trace + levels, LANES) if packed else (species, trace + levels, columns)
    edge, top, send = pl.pallas_call(
        offset_kernel,
        out_shape=(
            pltpu.HBM(edge_shape, F32),
            held((species, levels, trace, columns)),
            shape(send_shape),
        ),
        in_specs=[VMEM] * 10,
        out_specs=(HBM, VMEM, VMEM),
        scratch_shapes=[pltpu.VMEM(edge_shape, F32), pltpu.SemaphoreType.DMA((species,))],
        compiler_params=PARAMS,
        name="slab_offsets",
    )(
        rim, mid_top, types, inlet, a_top, c_all, right, left, from_left, from_right
    )
    part = columns // flow_n
    if not packed:
        send = send.reshape(species, trace + levels, flow_n, part)
        send = send.transpose(2, 1, 0, 3).reshape(flow_n, trace + levels, species * part)
    got = lax.all_to_all(send, "flow", 0, 0, tiled=True)

    outer_rest, coef = pl.pallas_call(
        rest_kernel,
        out_shape=(
            held((species, levels, rest, 2 * LANES)),
            held((types_n, trace, trace, species * part)),
        ),
        in_specs=[HBM] + [VMEM] * 3,
        out_specs=(VMEM, VMEM),
        scratch_shapes=[pltpu.VMEM(edge_shape, F32), pltpu.SemaphoreType.DMA((species,))],
        compiler_params=PARAMS,
        cost_estimate=cost(rest, columns),
        name="rest_sources",
    )(far(edge), types, a_rest, small)
    back = pl.pallas_call(
        owner_kernel,
        out_shape=shape((flow_n, trace, species * part)),
        in_specs=[VMEM, VMEM],
        out_specs=VMEM,
        compiler_params=PARAMS,
        name="owner_sweep",
    )(coef, got)
    traces = lax.all_to_all(back, "flow", 0, 0, tiled=True)
    if not packed:
        traces = traces.reshape(flow_n, trace, species, part)
        traces = traces.transpose(2, 1, 0, 3).reshape(species, trace, columns)

    return pl.pallas_call(
        final_kernel,
        out_shape=shape(conc_old.shape, BF16),
        in_specs=[VMEM] * 7,
        out_specs=HBM,
        scratch_shapes=[
            pltpu.VMEM(conc_old.shape, BF16),
            pltpu.SemaphoreType.DMA((pairs,)),
        ],
        compiler_params=PARAMS,
        name="final_sweep",
    )(top, inner_rest, outer_rest, types, inlet, c_all, traces)


def solution(mesh):
    in_specs = (
        P(None, "flow", None, "lat"),
        P("flow", "lat"),
        P("flow", "lat"),
        P(None, None, "lat"),
        P(),
    )
    out_specs = P(None, "flow", None, "lat")
    return jax.shard_map(
        on_device, mesh=mesh, in_specs=in_specs, out_specs=out_specs, check_vma=False
    )
```

```python
import jax
import jax.numpy as jnp
from jax import lax
from jax.experimental import pallas as pl
from jax.experimental.pallas import tpu as pltpu
from jax.sharding import PartitionSpec as P

F32 = jnp.float32
BF16 = jnp.bfloat16
VMEM = pl.BlockSpec(memory_space=pltpu.VMEM)
HBM = pl.BlockSpec(memory_space=pltpu.HBM)
LANES = 128
PARAMS = pltpu.CompilerParams(vmem_limit_bytes=20 << 20)


def lane_index(shape):
    return lax.broadcasted_iota(jnp.int32, shape, len(shape) - 1)


def split(x):
    hi = x.astype(BF16)
    return hi, (x - hi.astype(F32)).astype(BF16)


def stacked_parts(x):
    hi, lo = split(x)
    return jnp.concatenate([hi, lo, hi], axis=0)


def pick(per_type, types, rows):
    columns = per_type.shape[1]
    grid = per_type.reshape(-1, rows // 8, 8, columns)
    out = grid[0]
    for t in range(1, grid.shape[0]):
        out = jnp.where((types == t)[None], grid[t], out)
    return out.reshape(rows, columns)


def masked_parts(x, masks):
    hi, lo = split(x)
    parts = []
    for mask in masks:
        his = hi * mask
        parts += [his, lo * mask, his]
    return jnp.concatenate(parts, axis=0)


def masks_of(type_ref, level, types_n, rows):
    types = jnp.broadcast_to(type_ref[level : level + 1], (rows, type_ref.shape[1]))
    return [jnp.where(types == t, 1.0, 0.0).astype(BF16) for t in range(types_n)]


def mm(a, b):
    return jnp.dot(a, b, preferred_element_type=F32)


def pair_lane(s, l, species):
    return s * (LANES // species) + l


def placed(pieces, rows):
    lane = lane_index((rows, LANES))
    tile = jnp.zeros((rows, LANES), F32)
    for array, source, target, count in pieces:
        moved = pltpu.roll(array, (target - source) % LANES, 1) if target != source else array
        tile = jnp.where((lane >= target) & (lane < target + count), moved, tile)
    return tile


def summed(terms):
    while len(terms) > 1:
        terms = [a + b for a, b in zip(terms[::2], terms[1::2])]
    return terms[0]


def high_low(x):
    hi = x.astype(BF16).astype(F32)
    return hi, x - hi


def table_parts(table_ref, s, t):
    dofs, wide_n = table_ref.shape[2:]
    return high_low(jnp.concatenate([table_ref[s, t], jnp.zeros((dofs, LANES - wide_n), F32)], axis=1))


def source_rows(hi, lo, dofs):
    twice = jnp.where(lane_index(hi.shape) < dofs, hi, pltpu.roll(hi, dofs, 1))
    return jnp.concatenate([twice, lo[:, :dofs]], axis=1).astype(BF16)


def fill_top_tables(table_ref, a_top_ref, c1_ref, c2_ref, small_ref, coef_ref):
    species, types_n, dofs, _ = table_ref.shape
    trace = small_ref.shape[2]
    rest = dofs - trace
    share = LANES // species
    below = []
    for s in range(species):
        tops, single = [], []
        for t in range(types_n):
            hi, lo = (part[rest:] for part in table_parts(table_ref, s, t))
            small_ref[s, t] = table_ref[s, t, rest:, dofs:]
            tops.append(source_rows(hi, lo, dofs))
            pieces = [(hi, dofs, 0, trace), (hi, dofs, trace, trace), (lo, dofs, 2 * trace, trace)]
            single.append(placed(pieces, trace))
            below.append((hi + lo, dofs, s * share + t * trace, trace))
        a_top_ref[s] = jnp.concatenate(tops, axis=0)
        c1_ref[s] = jnp.concatenate(single, axis=0).astype(BF16)[:, : 3 * trace]
    fill_coefs(coef_ref, small_ref)
    below = placed(below, trace)
    products = []
    for t in range(types_n):
        terms = [coef_ref[t, k] * below[k : k + 1] for k in range(trace)]
        products.append(high_low(summed(terms)))
    for s in range(species):
        double = []
        for t in range(types_n):
            at = s * share + t * trace
            for hi, lo in products:
                pieces = [(hi, at, 0, trace), (hi, at, trace, trace), (lo, at, 2 * trace, trace)]
                double.append(placed(pieces, trace))
        c2_ref[s] = jnp.concatenate(double, axis=0).astype(BF16)[:, : 3 * trace]


def fill_late_tables(table_ref, a_rest_ref, c_ref):
    species, types_n, dofs, _ = table_ref.shape
    count = c_ref.shape[2]
    trace = count // (3 * types_n)
    rest = dofs - trace
    for s in range(species):
        parts = [table_parts(table_ref, s, t) for t in range(types_n)]
        a_rest_ref[s] = jnp.concatenate([source_rows(hi[:rest], lo[:rest], dofs) for hi, lo in parts], axis=0)
        tiles = []
        for start in range(0, count, LANES):
            pieces = []
            for at in range(start, min(count, start + LANES), trace):
                k = at // trace
                pieces.append((parts[k // 3][(0, 0, 1)[k % 3]], dofs, at - start, trace))
            tile = placed(pieces, dofs)
            tiles.append(jnp.concatenate([tile[rest:], tile[:rest]], axis=0).astype(BF16))
        c_ref[s] = jnp.concatenate(tiles, axis=1)[:, :count]


def load_kernel(
    conc_hbm, vel_hbm, type_hbm, table_hbm, inlet_hbm, x_ref, vel_ref, type_ref, table_ref, inlet_ref, right_ref, left_ref,
    sems, small_sems,
):
    species, tiles_n, levels, dofs, _ = x_ref.shape
    trace = right_ref.shape[0]
    stride = dofs // trace
    small = ((vel_hbm, vel_ref), (type_hbm, type_ref), (table_hbm, table_ref), (inlet_hbm, inlet_ref))
    small = [pltpu.make_async_copy(*ends, small_sems.at[i]) for i, ends in enumerate(small)]
    copies = []
    small[0].start()
    for i in [0, tiles_n - 1, *range(1, tiles_n - 1)]:
        for s in range(species):
            block = conc_hbm.at[s, :, :, pl.ds(i * LANES, LANES)]
            copies.append(pltpu.make_async_copy(block, x_ref.at[s, i], sems.at[s * tiles_n + i]))
            copies[-1].start()
    for copy in small[1:]:
        copy.start()
    small[0].wait()
    lane = lane_index((levels, LANES))
    on_diag = lane % (LANES // species) == lax.broadcasted_iota(jnp.int32, lane.shape, 0)
    face = jnp.broadcast_to(vel_ref[:, :1], (levels, LANES))
    face = jnp.sum(jnp.where(on_diag, face, 0.0), axis=0, keepdims=True)
    left_ref[trace:] = jnp.broadcast_to(face, (left_ref.shape[0] - trace, LANES))
    for copy in copies[: 2 * species]:
        copy.wait()
    lane = lane_index((trace, LANES))
    right = jnp.zeros((trace, LANES), F32)
    left = jnp.zeros((trace, LANES), F32)
    for s in range(species):
        for l in range(levels):
            p = pair_lane(s, l, species)
            last = x_ref[s, tiles_n - 1, l, pl.ds(stride - 1, trace, stride=stride), :]
            first = x_ref[s, 0, l, pl.ds(0, trace, stride=stride), :]
            right = jnp.where(lane == p, pltpu.roll(last, (p + 1) % LANES, 1), right)
            left = jnp.where(lane == p, pltpu.roll(first, p, 1) if p else first, left)
    right_ref[...] = right
    left_ref[:trace] = left
    for copy in copies[2 * species :] + small[1:]:
        copy.wait()


def fill_coefs(coef_ref, small_ref):
    types_n, trace, _, width = coef_ref.shape
    species = small_ref.shape[0]
    which = lane_index((trace, width)) // (width // species)
    for t in range(types_n):
        for j in range(trace):
            value = jnp.broadcast_to(small_ref[0, t, :, j : j + 1], (trace, width))
            for s in range(1, species):
                other = jnp.broadcast_to(small_ref[s, t, :, j : j + 1], (trace, width))
                value = jnp.where(which == s, other, value)
            coef_ref[t, j] = value


def two_levels(trace_in, c2_ref, s, types, trace):
    return pick(mm(c2_ref[s], stacked_parts(trace_in)), types, trace)


def one_level(trace_in, c1_ref, s, types, trace):
    return pick(mm(c1_ref[s], stacked_parts(trace_in)), types, trace)


def inner_kernel(
    x_ref, vel_ref, type_ref, table_ref, inlet_ref, source_hbm, mid_top_ref, offset_ref, a_top_ref, c1_ref, c2_ref,
    small_ref, coef_ref, source_ref, store_sems,
):
    species, levels, tiles_n, dofs, _ = source_ref.shape
    columns = tiles_n * LANES
    trace = inlet_ref.shape[1]
    types_n = small_ref.shape[1]
    stride = dofs // trace
    fill_top_tables(table_ref, a_top_ref, c1_ref, c2_ref, small_ref, coef_ref)
    lane = lane_index((trace, columns))
    zero, three = pl.ds(0, trace, stride=stride), pl.ds(stride - 1, trace, stride=stride)
    stores = []
    tops = [[] for _ in range(species)]
    traces = []
    start = (lax.axis_index("flow") == 0).astype(F32)
    for l in range(levels):
        velocity = jnp.broadcast_to(vel_ref[l : l + 1], (trace, columns))
        plus = jnp.where(lane > 0, jnp.maximum(velocity, 0.0), 0.0)
        minus = jnp.minimum(velocity, 0.0)
        types = jnp.broadcast_to(type_ref[l : l + 1], (8, columns))
        for s in range(species):
            views = [x_ref.at[s, i, l] for i in range(tiles_n)]
            low = jnp.concatenate([view[zero, :] for view in views], axis=1)
            high = jnp.concatenate([view[three, :] for view in views], axis=1)
            flux = plus * pltpu.roll(high, 1, 1) + minus * low
            out = jnp.where(lane == columns - 1, 0.0, pltpu.roll(flux, columns - 1, 1))
            low, high = low + flux, high - out
            for i, view in enumerate(views):
                source_ref[s, l, i] = view[...]
                source_ref[s, l, i, zero, :] = low[:, i * LANES : (i + 1) * LANES]
                source_ref[s, l, i, three, :] = high[:, i * LANES : (i + 1) * LANES]
            source = jnp.concatenate([source_ref[s, l, i] for i in range(tiles_n)], axis=1)
            top = pick(mm(a_top_ref[s], stacked_parts(source)), types, trace)
            tops[s].append(top)
            mid_top_ref[s, l] = top[:, LANES : columns - LANES]
        if l % 2:
            below = jnp.broadcast_to(type_ref[l - 1 : l], (8, columns))
            both = below * types_n + types
            for s in range(species):
                lower, upper = tops[s][-2:]
                if l == 1:
                    traces.append(inlet_ref[s] * start)
                added = one_level(lower, c1_ref, s, types, trace) + upper
                traces[s] = two_levels(traces[s], c2_ref, s, both, trace) + added
        if (l + 1) % (levels // 2) == 0:
            part = pl.ds(l + 1 - levels // 2, levels // 2)
            for s in range(species):
                ends = source_ref.at[s, part], source_hbm.at[s, part]
                stores.append(pltpu.make_async_copy(*ends, store_sems.at[len(stores)]))
                stores[-1].start()
    for s in range(species):
        offset_ref[s] = traces[s]
    for copy in stores:
        copy.wait()


def trace_step(state, types, coef_ref):
    types_n, trace = coef_ref.shape[:2]
    chosen = [types == float(t) for t in range(1, types_n)]
    terms = []
    for j in range(trace):
        coef = coef_ref[0, j]
        for t in range(1, types_n):
            coef = jnp.where(chosen[t - 1], coef_ref[t, j], coef)
        terms.append(coef * state[j : j + 1])
    return summed(terms)


def halo_kernel(
    offset_ref, type_ref, a_top_ref, coef_ref, own_right_ref, own_left_ref, from_left_ref, from_right_ref,
    send_ref, flux_ref, delta_ref,
):
    species, trace, columns = offset_ref.shape
    levels = type_ref.shape[0]
    dofs = delta_ref.shape[0]
    stride = dofs // trace
    lat, lat_n = lax.axis_index("lat"), lax.axis_size("lat")
    has_left = (lat > 0).astype(F32)
    has_right = (lat < lat_n - 1).astype(F32)
    far_edge = LANES // species // 2

    def face(ref):
        return jnp.broadcast_to(ref[trace : trace + 1], (trace, LANES))

    coming = jnp.maximum(face(own_left_ref), 0.0) * from_left_ref[...] * has_left
    velocity = face(from_right_ref)
    leaving = jnp.maximum(velocity, 0.0) * own_right_ref[...]
    leaving = -(leaving + jnp.minimum(velocity, 0.0) * from_right_ref[:trace]) * has_right
    flux_ref[0] = coming
    flux_ref[1] = leaving
    lane = lane_index((trace, LANES))
    within = lane % (LANES // species)
    near, far = within < levels, (within >= far_edge) & (within < far_edge + levels)
    delta_ref[...] = jnp.zeros((dofs, LANES), F32)
    delta_ref[pl.ds(0, trace, stride=stride), :] = jnp.where(near, coming, 0.0)
    delta_ref[pl.ds(stride - 1, trace, stride=stride), :] = jnp.where(
        far, pltpu.roll(leaving, far_edge, 1), 0.0
    )
    types = type_ref[...].astype(F32)
    sub = lax.broadcasted_iota(jnp.int32, (levels, LANES), 0)
    spot = lane_index((levels, LANES)) % (LANES // species)
    here = jnp.where(spot == sub, jnp.broadcast_to(types[:, :1], (levels, LANES)), 0.0)
    there = jnp.broadcast_to(types[:, columns - 1 :], (levels, LANES))
    here = here + jnp.where(spot == sub + far_edge, there, 0.0)
    edge_types = jnp.broadcast_to(jnp.sum(here, axis=0, keepdims=True), (trace, LANES))
    parts = stacked_parts(delta_ref[...])
    added = pick(mm(a_top_ref[0], parts), edge_types[:8], trace)
    for s in range(1, species):
        other = pick(mm(a_top_ref[s], parts), edge_types[:8], trace)
        added = jnp.where(lane < s * (LANES // species), added, other)
    state = added
    for l in range(1, levels):
        state = trace_step(state, pltpu.roll(edge_types, LANES - l, 1), coef_ref)
        state = state + pltpu.roll(added, LANES - l, 1)
    traces = []
    for s in range(species):
        at = pair_lane(s, 0, species)
        first = pltpu.roll(state, LANES - at, 1) if at else state
        last = pltpu.roll(state, LANES - 1 - at - far_edge, 1)
        first = offset_ref[s, :, :LANES] + jnp.where(lane == 0, first, 0.0)
        last = offset_ref[s, :, columns - LANES :] + jnp.where(lane == LANES - 1, last, 0.0)
        traces.append(jnp.concatenate([first, offset_ref[s, :, LANES : columns - LANES], last], axis=1))
    width = send_ref.shape[2]
    if width == LANES:
        half = width // 2
        low = lane_index((trace, width)) < half
        low_t = lane_index((levels, width)) < half
        for k in range(columns // width):
            a, b = (traces[s][:, k * width : (k + 1) * width] for s in (0, 1))
            t = types[:, k * width : (k + 1) * width]
            swapped = pltpu.roll(t, half, 1)
            send_ref[2 * k, :trace] = jnp.where(low, a, pltpu.roll(b, half, 1))
            send_ref[2 * k + 1, :trace] = jnp.where(low, pltpu.roll(a, half, 1), b)
            send_ref[2 * k, trace:] = jnp.where(low_t, t, swapped)
            send_ref[2 * k + 1, trace:] = jnp.where(low_t, swapped, t)
    else:
        for s in range(species):
            send_ref[s, :trace] = traces[s]
            send_ref[s, trace:] = types


def rest_kernel(
    source_hbm, flux_ref, type_ref, a_top_ref, table_ref, small_ref, rest_ref, edge_top_ref, c_ref, coef_ref, a_rest_ref,
    source_ref, sems,
):
    species, levels, tiles_n, dofs, _ = source_ref.shape
    columns = tiles_n * LANES
    rest = rest_ref.shape[2]
    trace = dofs - rest
    stride = dofs // trace
    copies = []
    for h in range(2):
        for s in range(species):
            part = pl.ds(h * (levels // 2), levels // 2)
            ends = source_hbm.at[s, part], source_ref.at[s, part]
            copies.append(pltpu.make_async_copy(*ends, sems.at[len(copies)]))
            copies[-1].start()
    fill_late_tables(table_ref, a_rest_ref, c_ref)
    fill_coefs(coef_ref, small_ref)
    lane = lane_index((trace, LANES))
    zero, three = pl.ds(0, trace, stride=stride), pl.ds(stride - 1, trace, stride=stride)
    for l in range(levels):
        types = jnp.broadcast_to(type_ref[l : l + 1], (8, columns))
        edge_types = jnp.concatenate([types[:, :LANES], types[:, columns - LANES :]], axis=1)
        if l % (levels // 2) == 0:
            for s in range(species):
                copies[(l // (levels // 2)) * species + s].wait()
        for s in range(species):
            p = pair_lane(s, l, species)
            first = pltpu.roll(flux_ref[0], (LANES - p) % LANES, 1)
            last = pltpu.roll(flux_ref[1], LANES - 1 - p, 1)
            end = tiles_n - 1
            low, high = source_ref[s, l, 0, zero, :], source_ref[s, l, end, three, :]
            source_ref[s, l, 0, zero, :] = low + jnp.where(lane == 0, first, 0.0)
            source_ref[s, l, end, three, :] = high + jnp.where(lane == LANES - 1, last, 0.0)
            parts = stacked_parts(jnp.concatenate([source_ref[s, l, i] for i in range(tiles_n)], axis=1))
            rest_ref[s, l] = pick(mm(a_rest_ref[s], parts), types, rest)
            outer = jnp.concatenate([parts[:, :LANES], parts[:, columns - LANES :]], axis=1)
            edge_top_ref[s, l] = pick(mm(a_top_ref[s], outer), edge_types, trace)


def owner_kernel(coef_ref, got_ref, out_ref):
    slabs, _, width = got_ref.shape
    trace = coef_ref.shape[1]
    levels = got_ref.shape[1] - trace
    out_ref[0] = jnp.zeros((trace, width), F32)

    def slab(g, state):
        out_ref[g] = state
        for l in range(levels):
            types = jnp.broadcast_to(got_ref[g, trace + l : trace + l + 1], (trace, width))
            state = trace_step(state, types, coef_ref)
        return state + got_ref[g, :trace]

    last = lax.fori_loop(1, slabs - 1, slab, got_ref[0, :trace])
    out_ref[slabs - 1] = last


def final_kernel(
    mid_top_ref, edge_top_ref, rest_ref, type_ref, inlet_ref, c_ref, c1_ref, c2_ref, got_ref, out_hbm, o_ref, sems
):
    species, levels, rest, columns = rest_ref.shape
    trace = inlet_ref.shape[1]
    types_n = c_ref.shape[2] // (3 * trace)
    width = got_ref.shape[2]
    is_first = lax.axis_index("flow") == 0
    if width == LANES:
        half = width // 2
        low = lane_index((trace, width)) < half
        tiles = [[], []]
        for k in range(columns // width):
            a, b = got_ref[2 * k], got_ref[2 * k + 1]
            tiles[0].append(jnp.where(low, a, pltpu.roll(b, half, 1)))
            tiles[1].append(jnp.where(low, pltpu.roll(a, half, 1), b))
        received = [jnp.concatenate(t, axis=1) for t in tiles]
    else:
        received = [got_ref[s] for s in range(species)]
    both = range(species)
    inflow = {(0, s): jnp.where(is_first, inlet_ref[s], received[s]) for s in both}
    types = [jnp.broadcast_to(type_ref[l : l + 1], (8, columns)) for l in range(levels)]

    def top(s, l):
        edge = edge_top_ref[s, l]
        return jnp.concatenate([edge[:, :LANES], mid_top_ref[s, l], edge[:, LANES:]], axis=1)

    added = {}
    for l in range(0, levels - 2, 2):
        for s in both:
            added[l, s] = one_level(top(s, l), c1_ref, s, types[l + 1], trace) + top(s, l + 1)
    copies = []

    def solve(l):
        masks = masks_of(type_ref, l, types_n, trace)
        for s in both:
            moved = mm(c_ref[s], masked_parts(inflow[l, s], masks))
            outflow = moved[:trace] + top(s, l)
            if l % 2 == 0:
                inflow[l + 1, s] = outflow
            o_ref[s, l, rest:] = outflow.astype(BF16)
            o_ref[s, l, :rest] = (moved[trace:] + rest_ref[s, l]).astype(BF16)
            copies.append(pltpu.make_async_copy(o_ref.at[s, l], out_hbm.at[s, l], sems.at[s * levels + l]))
            copies[-1].start()

    for l in range(0, levels, 2):
        if l + 2 < levels:
            for s in both:
                ahead = two_levels(inflow[l, s], c2_ref, s, types[l] * types_n + types[l + 1], trace)
                inflow[l + 2, s] = ahead + added[l, s]
        if l:
            solve(l - 1)
        solve(l)
    solve(levels - 1)
    for copy in copies:
        copy.wait()


def on_device(conc_old, lat_velocity, elem_type, inlet_trace, solve_table):
    species, levels, dofs, columns = conc_old.shape
    types_n = solve_table.shape[1]
    trace = inlet_trace.shape[1]
    flow_n = lax.axis_size("flow")
    lat_n = lax.axis_size("lat")
    pairs = species * levels
    tiles = columns // LANES
    inner = columns - 2 * LANES
    rest = dofs - trace

    def shape(dims, kind=F32):
        return jax.ShapeDtypeStruct(dims, kind)

    def held(dims, kind=F32):
        return pltpu.VMEM(dims, kind)

    def far(array):
        return pltpu.with_memory_space_constraint(array, pltpu.HBM)

    def cost(rows, count):
        flops = 2 * 3 * types_n * rows * dofs * count * pairs
        return pl.CostEstimate(
            flops=flops, bytes_accessed=8 * pairs * dofs * columns, transcendentals=0
        )

    x, velocity, types, table, inlet, right, left = pl.pallas_call(
        load_kernel,
        out_shape=(
            held((species, tiles, levels, dofs, LANES)),
            held(lat_velocity.shape),
            held(elem_type.shape, elem_type.dtype),
            held(solve_table.shape),
            held(inlet_trace.shape),
            shape((trace, LANES)),
            shape((trace + 8, LANES)),
        ),
        in_specs=[HBM] * 5,
        out_specs=(VMEM,) * 7,
        scratch_shapes=[pltpu.SemaphoreType.DMA((species * tiles,)), pltpu.SemaphoreType.DMA((4,))],
        compiler_params=PARAMS,
        name="load_edges",
    )(far(conc_old), far(lat_velocity), far(elem_type), far(solve_table), far(inlet_trace))
    from_left = lax.ppermute(right, "lat", [(i, (i + 1) % lat_n) for i in range(lat_n)])
    from_right = lax.ppermute(left, "lat", [((i + 1) % lat_n, i) for i in range(lat_n)])


    source_shape = (species, levels, tiles, dofs, LANES)
    source, mid_top, offset, a_top, c_one, c_two, small, coef = pl.pallas_call(
        inner_kernel,
        out_shape=(
            pltpu.HBM(source_shape, F32),
            held((species, levels, trace, inner)),
            held((species, trace, columns)),
            held((species, types_n * trace, 3 * dofs), BF16),
            held((species, types_n * trace, 3 * trace), BF16),
            held((species, types_n * types_n * trace, 3 * trace), BF16),
            held((species, types_n, trace, trace)),
            held((types_n, trace, trace, LANES)),
        ),
        in_specs=[VMEM] * 5,
        out_specs=(HBM,) + (VMEM,) * 7,
        scratch_shapes=[pltpu.VMEM(source_shape, F32), pltpu.SemaphoreType.DMA((2 * species,))],
        compiler_params=PARAMS,
        cost_estimate=cost(dofs, columns),
        name="inner_sources",
    )(x, velocity, types, table, inlet)

    packed = 2 * columns == LANES * flow_n and species == 2
    send_shape = (flow_n, trace + levels, LANES) if packed else (species, trace + levels, columns)
    send, flux = pl.pallas_call(
        halo_kernel,
        out_shape=(shape(send_shape), held((2, trace, LANES))),
        in_specs=[VMEM] * 8,
        out_specs=(VMEM, VMEM),
        scratch_shapes=[pltpu.VMEM((dofs, LANES), F32)],
        compiler_params=PARAMS,
        name="halo_offsets",
    )(offset, types, a_top, coef, right, left, from_left, from_right)
    part = columns // flow_n
    if not packed:
        send = send.reshape(species, trace + levels, flow_n, part)
        send = send.transpose(2, 1, 0, 3).reshape(flow_n, trace + levels, species * part)
    got = lax.all_to_all(send, "flow", 0, 0, tiled=True)

    rest_terms, edge_top, c_all, owner_coef = pl.pallas_call(
        rest_kernel,
        out_shape=(
            held((species, levels, rest, columns)),
            held((species, levels, trace, 2 * LANES)),
            held((species, dofs, 3 * types_n * trace), BF16),
            held((types_n, trace, trace, species * part)),
        ),
        in_specs=[HBM] + [VMEM] * 5,
        out_specs=(VMEM,) * 4,
        scratch_shapes=[
            pltpu.VMEM((species, types_n * rest, 3 * dofs), BF16),
            pltpu.VMEM(source_shape, F32),
            pltpu.SemaphoreType.DMA((2 * species,)),
        ],
        compiler_params=PARAMS,
        cost_estimate=cost(rest, columns),
        name="rest_sources",
    )(far(source), flux, types, a_top, table, small)
    back = pl.pallas_call(
        owner_kernel,
        out_shape=shape((flow_n, trace, species * part)),
        in_specs=[VMEM, VMEM],
        out_specs=VMEM,
        compiler_params=PARAMS,
        name="owner_sweep",
    )(owner_coef, got)
    traces = lax.all_to_all(back, "flow", 0, 0, tiled=True)
    if not packed:
        traces = traces.reshape(flow_n, trace, species, part)
        traces = traces.transpose(2, 1, 0, 3).reshape(species, trace, columns)

    return pl.pallas_call(
        final_kernel,
        out_shape=shape(conc_old.shape, BF16),
        in_specs=[VMEM] * 9,
        out_specs=HBM,
        scratch_shapes=[
            pltpu.VMEM(conc_old.shape, BF16),
            pltpu.SemaphoreType.DMA((pairs,)),
        ],
        compiler_params=PARAMS,
        name="final_sweep",
    )(mid_top, edge_top, rest_terms, types, inlet, c_all, c_one, c_two, traces)


def solution(mesh):
    in_specs = (
        P(None, "flow", None, "lat"),
        P("flow", "lat"),
        P("flow", "lat"),
        P(None, None, "lat"),
        P(),
    )
    out_specs = P(None, "flow", None, "lat")
    return jax.shard_map(
        on_device, mesh=mesh, in_specs=in_specs, out_specs=out_specs, check_vma=False
    )
```

```python
import jax
import jax.numpy as jnp
from jax import lax
from jax.experimental import pallas as pl
from jax.experimental.pallas import tpu as pltpu
from jax.sharding import PartitionSpec as P

F32 = jnp.float32
BF16 = jnp.bfloat16
VMEM = pl.BlockSpec(memory_space=pltpu.VMEM)
HBM = pl.BlockSpec(memory_space=pltpu.HBM)
LANES = 128
PARAMS = pltpu.CompilerParams(vmem_limit_bytes=20 << 20)


def lane_index(shape):
    return lax.broadcasted_iota(jnp.int32, shape, len(shape) - 1)


def split(x):
    hi = x.astype(BF16)
    return hi, (x - hi.astype(F32)).astype(BF16)


def stacked_parts(x):
    hi, lo = split(x)
    return jnp.concatenate([hi, lo, hi], axis=0)


def pick(per_type, types, rows):
    columns = per_type.shape[1]
    grid = per_type.reshape(-1, rows // 8, 8, columns)
    out = grid[0]
    for t in range(1, grid.shape[0]):
        out = jnp.where((types == t)[None], grid[t], out)
    return out.reshape(rows, columns)


def masked_parts(x, masks):
    hi, lo = split(x)
    parts = []
    for mask in masks:
        his = hi * mask
        parts += [his, lo * mask, his]
    return jnp.concatenate(parts, axis=0)


def masks_of(type_ref, level, types_n, rows):
    types = jnp.broadcast_to(type_ref[level : level + 1], (rows, type_ref.shape[1]))
    return [jnp.where(types == t, 1.0, 0.0).astype(BF16) for t in range(types_n)]


def mm(a, b):
    return jnp.dot(a, b, preferred_element_type=F32)


def pair_lane(s, l, species):
    return s * (LANES // species) + l


def placed(pieces, rows):
    lane = lane_index((rows, LANES))
    tile = jnp.zeros((rows, LANES), F32)
    for array, source, target, count in pieces:
        moved = pltpu.roll(array, (target - source) % LANES, 1) if target != source else array
        tile = jnp.where((lane >= target) & (lane < target + count), moved, tile)
    return tile


def summed(terms):
    while len(terms) > 1:
        terms = [a + b for a, b in zip(terms[::2], terms[1::2])]
    return terms[0]


def high_low(x):
    hi = x.astype(BF16).astype(F32)
    return hi, x - hi


def table_parts(table_ref, s, t):
    dofs, wide_n = table_ref.shape[2:]
    return high_low(jnp.concatenate([table_ref[s, t], jnp.zeros((dofs, LANES - wide_n), F32)], axis=1))


def source_rows(hi, lo, dofs):
    twice = jnp.where(lane_index(hi.shape) < dofs, hi, pltpu.roll(hi, dofs, 1))
    return jnp.concatenate([twice, lo[:, :dofs]], axis=1).astype(BF16)


def fill_top_tables(table_ref, a_top_ref, c1_ref, c2_ref, small_ref, coef_ref):
    species, types_n, dofs, _ = table_ref.shape
    trace = small_ref.shape[2]
    rest = dofs - trace
    share = LANES // species
    below = []
    for s in range(species):
        tops, single = [], []
        for t in range(types_n):
            hi, lo = (part[rest:] for part in table_parts(table_ref, s, t))
            small_ref[s, t] = table_ref[s, t, rest:, dofs:]
            tops.append(source_rows(hi, lo, dofs))
            pieces = [(hi, dofs, 0, trace), (hi, dofs, trace, trace), (lo, dofs, 2 * trace, trace)]
            single.append(placed(pieces, trace))
            below.append((hi + lo, dofs, s * share + t * trace, trace))
        a_top_ref[s] = jnp.concatenate(tops, axis=0)
        c1_ref[s] = jnp.concatenate(single, axis=0).astype(BF16)[:, : 3 * trace]
    fill_coefs(coef_ref, small_ref)
    below = placed(below, trace)
    products = []
    for t in range(types_n):
        terms = [coef_ref[t, k] * below[k : k + 1] for k in range(trace)]
        products.append(high_low(summed(terms)))
    for s in range(species):
        double = []
        for t in range(types_n):
            at = s * share + t * trace
            for hi, lo in products:
                pieces = [(hi, at, 0, trace), (hi, at, trace, trace), (lo, at, 2 * trace, trace)]
                double.append(placed(pieces, trace))
        c2_ref[s] = jnp.concatenate(double, axis=0).astype(BF16)[:, : 3 * trace]


def fill_late_tables(table_ref, a_rest_ref, c_ref):
    species, types_n, dofs, _ = table_ref.shape
    count = c_ref.shape[2]
    trace = count // (3 * types_n)
    rest = dofs - trace
    for s in range(species):
        parts = [table_parts(table_ref, s, t) for t in range(types_n)]
        a_rest_ref[s] = jnp.concatenate([source_rows(hi[:rest], lo[:rest], dofs) for hi, lo in parts], axis=0)
        tiles = []
        for start in range(0, count, LANES):
            pieces = []
            for at in range(start, min(count, start + LANES), trace):
                k = at // trace
                pieces.append((parts[k // 3][(0, 0, 1)[k % 3]], dofs, at - start, trace))
            tile = placed(pieces, dofs)
            tiles.append(jnp.concatenate([tile[rest:], tile[:rest]], axis=0).astype(BF16))
        c_ref[s] = jnp.concatenate(tiles, axis=1)[:, :count]


def load_kernel(
    conc_hbm, vel_hbm, type_hbm, table_hbm, inlet_hbm, x_ref, vel_ref, type_ref, table_ref, inlet_ref, right_ref, left_ref,
    near_ref, far_ref, sems, small_sems,
):
    species, tiles_n, levels, dofs, _ = x_ref.shape
    trace = right_ref.shape[0]
    stride = dofs // trace
    small = ((vel_hbm, vel_ref), (type_hbm, type_ref), (table_hbm, table_ref), (inlet_hbm, inlet_ref))
    small = [pltpu.make_async_copy(*ends, small_sems.at[i]) for i, ends in enumerate(small)]
    copies = []
    small[0].start()
    for i in [0, tiles_n - 1, *range(1, tiles_n - 1)]:
        for s in range(species):
            block = conc_hbm.at[s, :, :, pl.ds(i * LANES, LANES)]
            copies.append(pltpu.make_async_copy(block, x_ref.at[s, i], sems.at[s * tiles_n + i]))
            copies[-1].start()
    for copy in small[1:]:
        copy.start()
    small[0].wait()
    lane = lane_index((levels, LANES))
    on_diag = lane % (LANES // species) == lax.broadcasted_iota(jnp.int32, lane.shape, 0)
    face = jnp.broadcast_to(vel_ref[:, :1], (levels, LANES))
    face = jnp.sum(jnp.where(on_diag, face, 0.0), axis=0, keepdims=True)
    left_ref[trace:] = jnp.broadcast_to(face, (left_ref.shape[0] - trace, LANES))
    for copy in copies[: 2 * species]:
        copy.wait()
    lane = lane_index((trace, LANES))
    right = jnp.zeros((trace, LANES), F32)
    left = jnp.zeros((trace, LANES), F32)
    for s in range(species):
        for l in range(levels):
            p = pair_lane(s, l, species)
            last = x_ref[s, tiles_n - 1, l, pl.ds(stride - 1, trace, stride=stride), :]
            first = x_ref[s, 0, l, pl.ds(0, trace, stride=stride), :]
            right = jnp.where(lane == p, pltpu.roll(last, (p + 1) % LANES, 1), right)
            left = jnp.where(lane == p, pltpu.roll(first, p, 1) if p else first, left)
    right_ref[...] = right
    left_ref[:trace] = left
    is_even = lax.axis_index("lat") % 2 == 0
    near_ref[:trace] = jnp.where(is_even, right, left)
    far_ref[:trace] = jnp.where(is_even, left, right)
    near_ref[trace:] = left_ref[trace:]
    far_ref[trace:] = left_ref[trace:]
    for copy in copies[2 * species :] + small[1:]:
        copy.wait()


def fill_coefs(coef_ref, small_ref):
    types_n, trace, _, width = coef_ref.shape
    species = small_ref.shape[0]
    which = lane_index((trace, width)) // (width // species)
    for t in range(types_n):
        for j in range(trace):
            value = jnp.broadcast_to(small_ref[0, t, :, j : j + 1], (trace, width))
            for s in range(1, species):
                other = jnp.broadcast_to(small_ref[s, t, :, j : j + 1], (trace, width))
                value = jnp.where(which == s, other, value)
            coef_ref[t, j] = value


def two_levels(trace_in, c2_ref, s, types, trace):
    return pick(mm(c2_ref[s], stacked_parts(trace_in)), types, trace)


def one_level(trace_in, c1_ref, s, types, trace):
    return pick(mm(c1_ref[s], stacked_parts(trace_in)), types, trace)


def inner_kernel(
    x_ref, vel_ref, type_ref, table_ref, inlet_ref, source_hbm, mid_top_ref, offset_ref, a_top_ref, c1_ref, c2_ref,
    small_ref, coef_ref, source_ref, store_sems,
):
    species, levels, tiles_n, dofs, _ = source_ref.shape
    columns = tiles_n * LANES
    trace = inlet_ref.shape[1]
    types_n = small_ref.shape[1]
    stride = dofs // trace
    fill_top_tables(table_ref, a_top_ref, c1_ref, c2_ref, small_ref, coef_ref)
    lane = lane_index((trace, columns))
    zero, three = pl.ds(0, trace, stride=stride), pl.ds(stride - 1, trace, stride=stride)
    stores = []
    tops = [[] for _ in range(species)]
    traces = []
    start = (lax.axis_index("flow") == 0).astype(F32)
    for l in range(levels):
        velocity = jnp.broadcast_to(vel_ref[l : l + 1], (trace, columns))
        plus = jnp.where(lane > 0, jnp.maximum(velocity, 0.0), 0.0)
        minus = jnp.minimum(velocity, 0.0)
        types = jnp.broadcast_to(type_ref[l : l + 1], (8, columns))
        for s in range(species):
            views = [x_ref.at[s, i, l] for i in range(tiles_n)]
            low = jnp.concatenate([view[zero, :] for view in views], axis=1)
            high = jnp.concatenate([view[three, :] for view in views], axis=1)
            flux = plus * pltpu.roll(high, 1, 1) + minus * low
            out = jnp.where(lane == columns - 1, 0.0, pltpu.roll(flux, columns - 1, 1))
            low, high = low + flux, high - out
            for i, view in enumerate(views):
                source_ref[s, l, i] = view[...]
                source_ref[s, l, i, zero, :] = low[:, i * LANES : (i + 1) * LANES]
                source_ref[s, l, i, three, :] = high[:, i * LANES : (i + 1) * LANES]
            source = jnp.concatenate([source_ref[s, l, i] for i in range(tiles_n)], axis=1)
            top = pick(mm(a_top_ref[s], stacked_parts(source)), types, trace)
            tops[s].append(top)
            mid_top_ref[s, l] = top[:, LANES : columns - LANES]
        if l % 2:
            below = jnp.broadcast_to(type_ref[l - 1 : l], (8, columns))
            both = below * types_n + types
            for s in range(species):
                lower, upper = tops[s][-2:]
                if l == 1:
                    traces.append(inlet_ref[s] * start)
                added = one_level(lower, c1_ref, s, types, trace) + upper
                traces[s] = two_levels(traces[s], c2_ref, s, both, trace) + added
        if (l + 1) % (levels // 2) == 0:
            part = pl.ds(l + 1 - levels // 2, levels // 2)
            for s in range(species):
                ends = source_ref.at[s, part], source_hbm.at[s, part]
                stores.append(pltpu.make_async_copy(*ends, store_sems.at[len(stores)]))
                stores[-1].start()
    for s in range(species):
        offset_ref[s] = traces[s]
    for copy in stores:
        copy.wait()


def trace_step(state, types, coef_ref):
    types_n, trace = coef_ref.shape[:2]
    chosen = [types == float(t) for t in range(1, types_n)]
    terms = []
    for j in range(trace):
        coef = coef_ref[0, j]
        for t in range(1, types_n):
            coef = jnp.where(chosen[t - 1], coef_ref[t, j], coef)
        terms.append(coef * state[j : j + 1])
    return summed(terms)


def halo_kernel(
    offset_ref, type_ref, a_top_ref, coef_ref, own_right_ref, own_left_ref, near_ref, far_ref,
    send_ref, flux_ref, delta_ref,
):
    species, trace, columns = offset_ref.shape
    levels = type_ref.shape[0]
    dofs = delta_ref.shape[0]
    stride = dofs // trace
    lat, lat_n = lax.axis_index("lat"), lax.axis_size("lat")
    has_left = (lat > 0).astype(F32)
    has_right = (lat < lat_n - 1).astype(F32)
    far_edge = LANES // species // 2

    def face(ref):
        return jnp.broadcast_to(ref[trace : trace + 1], (trace, LANES))

    is_even = lat % 2 == 0
    from_left = jnp.where(is_even, far_ref[:trace], near_ref[:trace])
    from_right = jnp.where(is_even, near_ref[:trace], far_ref[:trace])
    coming = jnp.maximum(face(own_left_ref), 0.0) * from_left * has_left
    velocity = jnp.where(is_even, face(near_ref), face(far_ref))
    leaving = jnp.maximum(velocity, 0.0) * own_right_ref[...]
    leaving = -(leaving + jnp.minimum(velocity, 0.0) * from_right) * has_right
    flux_ref[0] = coming
    flux_ref[1] = leaving
    lane = lane_index((trace, LANES))
    within = lane % (LANES // species)
    near, far = within < levels, (within >= far_edge) & (within < far_edge + levels)
    delta_ref[...] = jnp.zeros((dofs, LANES), F32)
    delta_ref[pl.ds(0, trace, stride=stride), :] = jnp.where(near, coming, 0.0)
    delta_ref[pl.ds(stride - 1, trace, stride=stride), :] = jnp.where(
        far, pltpu.roll(leaving, far_edge, 1), 0.0
    )
    types = type_ref[...].astype(F32)
    sub = lax.broadcasted_iota(jnp.int32, (levels, LANES), 0)
    spot = lane_index((levels, LANES)) % (LANES // species)
    here = jnp.where(spot == sub, jnp.broadcast_to(types[:, :1], (levels, LANES)), 0.0)
    there = jnp.broadcast_to(types[:, columns - 1 :], (levels, LANES))
    here = here + jnp.where(spot == sub + far_edge, there, 0.0)
    edge_types = jnp.broadcast_to(jnp.sum(here, axis=0, keepdims=True), (trace, LANES))
    parts = stacked_parts(delta_ref[...])
    added = pick(mm(a_top_ref[0], parts), edge_types[:8], trace)
    for s in range(1, species):
        other = pick(mm(a_top_ref[s], parts), edge_types[:8], trace)
        added = jnp.where(lane < s * (LANES // species), added, other)
    state = added
    for l in range(1, levels):
        state = trace_step(state, pltpu.roll(edge_types, LANES - l, 1), coef_ref)
        state = state + pltpu.roll(added, LANES - l, 1)
    traces = []
    for s in range(species):
        at = pair_lane(s, 0, species)
        first = pltpu.roll(state, LANES - at, 1) if at else state
        last = pltpu.roll(state, LANES - 1 - at - far_edge, 1)
        first = offset_ref[s, :, :LANES] + jnp.where(lane == 0, first, 0.0)
        last = offset_ref[s, :, columns - LANES :] + jnp.where(lane == LANES - 1, last, 0.0)
        traces.append(jnp.concatenate([first, offset_ref[s, :, LANES : columns - LANES], last], axis=1))
    width = send_ref.shape[2]
    if width == LANES:
        half = width // 2
        low = lane_index((trace, width)) < half
        low_t = lane_index((levels, width)) < half
        for k in range(columns // width):
            a, b = (traces[s][:, k * width : (k + 1) * width] for s in (0, 1))
            t = types[:, k * width : (k + 1) * width]
            swapped = pltpu.roll(t, half, 1)
            send_ref[2 * k, :trace] = jnp.where(low, a, pltpu.roll(b, half, 1))
            send_ref[2 * k + 1, :trace] = jnp.where(low, pltpu.roll(a, half, 1), b)
            send_ref[2 * k, trace:] = jnp.where(low_t, t, swapped)
            send_ref[2 * k + 1, trace:] = jnp.where(low_t, swapped, t)
    else:
        for s in range(species):
            send_ref[s, :trace] = traces[s]
            send_ref[s, trace:] = types


def rest_kernel(
    source_hbm, flux_ref, type_ref, a_top_ref, table_ref, small_ref, rest_ref, edge_top_ref, c_ref, coef_ref, a_rest_ref,
    source_ref, sems,
):
    species, levels, tiles_n, dofs, _ = source_ref.shape
    columns = tiles_n * LANES
    rest = rest_ref.shape[2]
    trace = dofs - rest
    stride = dofs // trace
    copies = []
    for h in range(2):
        for s in range(species):
            part = pl.ds(h * (levels // 2), levels // 2)
            ends = source_hbm.at[s, part], source_ref.at[s, part]
            copies.append(pltpu.make_async_copy(*ends, sems.at[len(copies)]))
            copies[-1].start()
    fill_late_tables(table_ref, a_rest_ref, c_ref)
    fill_coefs(coef_ref, small_ref)
    lane = lane_index((trace, LANES))
    zero, three = pl.ds(0, trace, stride=stride), pl.ds(stride - 1, trace, stride=stride)
    for l in range(levels):
        types = jnp.broadcast_to(type_ref[l : l + 1], (8, columns))
        edge_types = jnp.concatenate([types[:, :LANES], types[:, columns - LANES :]], axis=1)
        if l % (levels // 2) == 0:
            for s in range(species):
                copies[(l // (levels // 2)) * species + s].wait()
        for s in range(species):
            p = pair_lane(s, l, species)
            first = pltpu.roll(flux_ref[0], (LANES - p) % LANES, 1)
            last = pltpu.roll(flux_ref[1], LANES - 1 - p, 1)
            end = tiles_n - 1
            low, high = source_ref[s, l, 0, zero, :], source_ref[s, l, end, three, :]
            source_ref[s, l, 0, zero, :] = low + jnp.where(lane == 0, first, 0.0)
            source_ref[s, l, end, three, :] = high + jnp.where(lane == LANES - 1, last, 0.0)
            parts = stacked_parts(jnp.concatenate([source_ref[s, l, i] for i in range(tiles_n)], axis=1))
            rest_ref[s, l] = pick(mm(a_rest_ref[s], parts), types, rest)
            outer = jnp.concatenate([parts[:, :LANES], parts[:, columns - LANES :]], axis=1)
            edge_top_ref[s, l] = pick(mm(a_top_ref[s], outer), edge_types, trace)


def owner_kernel(coef_ref, got_ref, out_ref):
    slabs, _, width = got_ref.shape
    trace = coef_ref.shape[1]
    levels = got_ref.shape[1] - trace
    out_ref[0] = jnp.zeros((trace, width), F32)

    def slab(g, state):
        out_ref[g] = state
        for l in range(levels):
            types = jnp.broadcast_to(got_ref[g, trace + l : trace + l + 1], (trace, width))
            state = trace_step(state, types, coef_ref)
        return state + got_ref[g, :trace]

    last = lax.fori_loop(1, slabs - 1, slab, got_ref[0, :trace])
    out_ref[slabs - 1] = last


def final_kernel(
    mid_top_ref, edge_top_ref, rest_ref, type_ref, inlet_ref, c_ref, c1_ref, c2_ref, got_ref, out_hbm, o_ref, sems
):
    species, levels, rest, columns = rest_ref.shape
    trace = inlet_ref.shape[1]
    types_n = c_ref.shape[2] // (3 * trace)
    width = got_ref.shape[2]
    is_first = lax.axis_index("flow") == 0
    if width == LANES:
        half = width // 2
        low = lane_index((trace, width)) < half
        tiles = [[], []]
        for k in range(columns // width):
            a, b = got_ref[2 * k], got_ref[2 * k + 1]
            tiles[0].append(jnp.where(low, a, pltpu.roll(b, half, 1)))
            tiles[1].append(jnp.where(low, pltpu.roll(a, half, 1), b))
        received = [jnp.concatenate(t, axis=1) for t in tiles]
    else:
        received = [got_ref[s] for s in range(species)]
    both = range(species)
    inflow = {(0, s): jnp.where(is_first, inlet_ref[s], received[s]) for s in both}
    types = [jnp.broadcast_to(type_ref[l : l + 1], (8, columns)) for l in range(levels)]

    def top(s, l):
        edge = edge_top_ref[s, l]
        return jnp.concatenate([edge[:, :LANES], mid_top_ref[s, l], edge[:, LANES:]], axis=1)

    added = {}
    for l in range(0, levels - 2, 2):
        for s in both:
            added[l, s] = one_level(top(s, l), c1_ref, s, types[l + 1], trace) + top(s, l + 1)
    copies = []

    def solve(l):
        masks = masks_of(type_ref, l, types_n, trace)
        for s in both:
            moved = mm(c_ref[s], masked_parts(inflow[l, s], masks))
            outflow = moved[:trace] + top(s, l)
            if l % 2 == 0:
                inflow[l + 1, s] = outflow
            o_ref[s, l, rest:] = outflow.astype(BF16)
            o_ref[s, l, :rest] = (moved[trace:] + rest_ref[s, l]).astype(BF16)
            copies.append(pltpu.make_async_copy(o_ref.at[s, l], out_hbm.at[s, l], sems.at[s * levels + l]))
            copies[-1].start()

    for l in range(0, levels, 2):
        if l + 2 < levels:
            for s in both:
                ahead = two_levels(inflow[l, s], c2_ref, s, types[l] * types_n + types[l + 1], trace)
                inflow[l + 2, s] = ahead + added[l, s]
        if l:
            solve(l - 1)
        solve(l)
    solve(levels - 1)
    for copy in copies:
        copy.wait()


def on_device(conc_old, lat_velocity, elem_type, inlet_trace, solve_table):
    species, levels, dofs, columns = conc_old.shape
    types_n = solve_table.shape[1]
    trace = inlet_trace.shape[1]
    flow_n = lax.axis_size("flow")
    lat_n = lax.axis_size("lat")
    pairs = species * levels
    tiles = columns // LANES
    inner = columns - 2 * LANES
    rest = dofs - trace

    def shape(dims, kind=F32):
        return jax.ShapeDtypeStruct(dims, kind)

    def held(dims, kind=F32):
        return pltpu.VMEM(dims, kind)

    def far(array):
        return pltpu.with_memory_space_constraint(array, pltpu.HBM)

    def cost(rows, count):
        flops = 2 * 3 * types_n * rows * dofs * count * pairs
        return pl.CostEstimate(
            flops=flops, bytes_accessed=8 * pairs * dofs * columns, transcendentals=0
        )

    x, velocity, types, table, inlet, right, left, near, far_side = pl.pallas_call(
        load_kernel,
        out_shape=(
            held((species, tiles, levels, dofs, LANES)),
            held(lat_velocity.shape),
            held(elem_type.shape, elem_type.dtype),
            held(solve_table.shape),
            held(inlet_trace.shape),
            held((trace, LANES)),
            held((trace + 8, LANES)),
            shape((trace + 8, LANES)),
            shape((trace + 8, LANES)),
        ),
        in_specs=[HBM] * 5,
        out_specs=(VMEM,) * 9,
        scratch_shapes=[pltpu.SemaphoreType.DMA((species * tiles,)), pltpu.SemaphoreType.DMA((4,))],
        compiler_params=PARAMS,
        name="load_edges",
    )(far(conc_old), far(lat_velocity), far(elem_type), far(solve_table), far(inlet_trace))
    assert lat_n % 2 == 0
    near_got = lax.ppermute(near, "lat", [(i, i ^ 1) for i in range(lat_n)])
    swap = [(i, (i - 1) % lat_n if i % 2 == 0 else (i + 1) % lat_n) for i in range(lat_n)]
    swap = [(i, j) for i, j in swap if abs(i - j) == 1]
    far_got = lax.ppermute(far_side, "lat", swap)


    source_shape = (species, levels, tiles, dofs, LANES)
    source, mid_top, offset, a_top, c_one, c_two, small, coef = pl.pallas_call(
        inner_kernel,
        out_shape=(
            pltpu.HBM(source_shape, F32),
            held((species, levels, trace, inner)),
            held((species, trace, columns)),
            held((species, types_n * trace, 3 * dofs), BF16),
            held((species, types_n * trace, 3 * trace), BF16),
            held((species, types_n * types_n * trace, 3 * trace), BF16),
            held((species, types_n, trace, trace)),
            held((types_n, trace, trace, LANES)),
        ),
        in_specs=[VMEM] * 5,
        out_specs=(HBM,) + (VMEM,) * 7,
        scratch_shapes=[pltpu.VMEM(source_shape, F32), pltpu.SemaphoreType.DMA((2 * species,))],
        compiler_params=PARAMS,
        cost_estimate=cost(dofs, columns),
        name="inner_sources",
    )(x, velocity, types, table, inlet)

    packed = 2 * columns == LANES * flow_n and species == 2
    send_shape = (flow_n, trace + levels, LANES) if packed else (species, trace + levels, columns)
    send, flux = pl.pallas_call(
        halo_kernel,
        out_shape=(shape(send_shape), held((2, trace, LANES))),
        in_specs=[VMEM] * 8,
        out_specs=(VMEM, VMEM),
        scratch_shapes=[pltpu.VMEM((dofs, LANES), F32)],
        compiler_params=PARAMS,
        name="halo_offsets",
    )(offset, types, a_top, coef, right, left, near_got, far_got)
    part = columns // flow_n
    if not packed:
        send = send.reshape(species, trace + levels, flow_n, part)
        send = send.transpose(2, 1, 0, 3).reshape(flow_n, trace + levels, species * part)
    got = lax.all_to_all(send, "flow", 0, 0, tiled=True)

    rest_terms, edge_top, c_all, owner_coef = pl.pallas_call(
        rest_kernel,
        out_shape=(
            held((species, levels, rest, columns)),
            held((species, levels, trace, 2 * LANES)),
            held((species, dofs, 3 * types_n * trace), BF16),
            held((types_n, trace, trace, species * part)),
        ),
        in_specs=[HBM] + [VMEM] * 5,
        out_specs=(VMEM,) * 4,
        scratch_shapes=[
            pltpu.VMEM((species, types_n * rest, 3 * dofs), BF16),
            pltpu.VMEM(source_shape, F32),
            pltpu.SemaphoreType.DMA((2 * species,)),
        ],
        compiler_params=PARAMS,
        cost_estimate=cost(rest, columns),
        name="rest_sources",
    )(far(source), flux, types, a_top, table, small)
    back = pl.pallas_call(
        owner_kernel,
        out_shape=shape((flow_n, trace, species * part)),
        in_specs=[VMEM, VMEM],
        out_specs=VMEM,
        compiler_params=PARAMS,
        name="owner_sweep",
    )(owner_coef, got)
    traces = lax.all_to_all(back, "flow", 0, 0, tiled=True)
    if not packed:
        traces = traces.reshape(flow_n, trace, species, part)
        traces = traces.transpose(2, 1, 0, 3).reshape(species, trace, columns)

    return pl.pallas_call(
        final_kernel,
        out_shape=shape(conc_old.shape, BF16),
        in_specs=[VMEM] * 9,
        out_specs=HBM,
        scratch_shapes=[
            pltpu.VMEM(conc_old.shape, BF16),
            pltpu.SemaphoreType.DMA((pairs,)),
        ],
        compiler_params=PARAMS,
        name="final_sweep",
    )(mid_top, edge_top, rest_terms, types, inlet, c_all, c_one, c_two, traces)


def solution(mesh):
    in_specs = (
        P(None, "flow", None, "lat"),
        P("flow", "lat"),
        P("flow", "lat"),
        P(None, None, "lat"),
        P(),
    )
    out_specs = P(None, "flow", None, "lat")
    return jax.shard_map(
        on_device, mesh=mesh, in_specs=in_specs, out_specs=out_specs, check_vma=False
    )
```

```python
import functools

import jax
import jax.numpy as jnp
from jax import lax
from jax.experimental import pallas as pl
from jax.experimental.pallas import tpu as pltpu
from jax.sharding import PartitionSpec as P

F32 = jnp.float32
BF16 = jnp.bfloat16
VMEM = pl.BlockSpec(memory_space=pltpu.VMEM)
HBM = pl.BlockSpec(memory_space=pltpu.HBM)
LANES = 128
PARAMS = pltpu.CompilerParams(vmem_limit_bytes=20 << 20)


def lane_index(shape):
    return lax.broadcasted_iota(jnp.int32, shape, len(shape) - 1)


def split(x):
    hi = x.astype(BF16)
    return hi, (x - hi.astype(F32)).astype(BF16)


def stacked_parts(x):
    hi, lo = split(x)
    return jnp.concatenate([hi, lo, hi], axis=0)


def pick(per_type, types, rows):
    columns = per_type.shape[1]
    grid = per_type.reshape(-1, rows // 8, 8, columns)
    out = grid[0]
    for t in range(1, grid.shape[0]):
        out = jnp.where((types == t)[None], grid[t], out)
    return out.reshape(rows, columns)


def masked_parts(x, masks):
    hi, lo = split(x)
    parts = []
    for mask in masks:
        his = hi * mask
        parts += [his, lo * mask, his]
    return jnp.concatenate(parts, axis=0)


def masks_of(type_ref, level, types_n, rows):
    types = jnp.broadcast_to(type_ref[level : level + 1], (rows, type_ref.shape[1]))
    return [jnp.where(types == t, 1.0, 0.0).astype(BF16) for t in range(types_n)]


def mm(a, b):
    return jnp.dot(a, b, preferred_element_type=F32)


def pair_lane(s, l, species):
    return s * (LANES // species) + l


def placed(pieces, rows):
    lane = lane_index((rows, LANES))
    tile = jnp.zeros((rows, LANES), F32)
    for array, source, target, count in pieces:
        moved = pltpu.roll(array, (target - source) % LANES, 1) if target != source else array
        tile = jnp.where((lane >= target) & (lane < target + count), moved, tile)
    return tile


def summed(terms):
    while len(terms) > 1:
        terms = [a + b for a, b in zip(terms[::2], terms[1::2])]
    return terms[0]


def high_low(x):
    hi = x.astype(BF16).astype(F32)
    return hi, x - hi


def table_parts(table_ref, s, t):
    dofs, wide_n = table_ref.shape[2:]
    return high_low(jnp.concatenate([table_ref[s, t], jnp.zeros((dofs, LANES - wide_n), F32)], axis=1))


def source_rows(hi, lo, dofs):
    twice = jnp.where(lane_index(hi.shape) < dofs, hi, pltpu.roll(hi, dofs, 1))
    return jnp.concatenate([twice, lo[:, :dofs]], axis=1).astype(BF16)


def fill_top_tables(table_ref, a_top_ref, c1_ref, c2_ref, small_ref, coef_ref):
    species, types_n, dofs, _ = table_ref.shape
    trace = small_ref.shape[2]
    rest = dofs - trace
    share = LANES // species
    below = []
    for s in range(species):
        tops, single = [], []
        for t in range(types_n):
            hi, lo = (part[rest:] for part in table_parts(table_ref, s, t))
            small_ref[s, t] = table_ref[s, t, rest:, dofs:]
            tops.append(source_rows(hi, lo, dofs))
            pieces = [(hi, dofs, 0, trace), (hi, dofs, trace, trace), (lo, dofs, 2 * trace, trace)]
            single.append(placed(pieces, trace))
            below.append((hi + lo, dofs, s * share + t * trace, trace))
        a_top_ref[s] = jnp.concatenate(tops, axis=0)
        c1_ref[s] = jnp.concatenate(single, axis=0).astype(BF16)[:, : 3 * trace]
    fill_coefs(coef_ref, small_ref)
    below = placed(below, trace)
    products = []
    for t in range(types_n):
        terms = [coef_ref[t, k] * below[k : k + 1] for k in range(trace)]
        products.append(high_low(summed(terms)))
    for s in range(species):
        double = []
        for t in range(types_n):
            at = s * share + t * trace
            for hi, lo in products:
                pieces = [(hi, at, 0, trace), (hi, at, trace, trace), (lo, at, 2 * trace, trace)]
                double.append(placed(pieces, trace))
        c2_ref[s] = jnp.concatenate(double, axis=0).astype(BF16)[:, : 3 * trace]


def fill_late_tables(table_ref, a_rest_ref, c_ref):
    species, types_n, dofs, _ = table_ref.shape
    count = c_ref.shape[2]
    trace = count // (3 * types_n)
    rest = dofs - trace
    for s in range(species):
        parts = [table_parts(table_ref, s, t) for t in range(types_n)]
        a_rest_ref[s] = jnp.concatenate([source_rows(hi[:rest], lo[:rest], dofs) for hi, lo in parts], axis=0)
        tiles = []
        for start in range(0, count, LANES):
            pieces = []
            for at in range(start, min(count, start + LANES), trace):
                k = at // trace
                pieces.append((parts[k // 3][(0, 0, 1)[k % 3]], dofs, at - start, trace))
            tile = placed(pieces, dofs)
            tiles.append(jnp.concatenate([tile[rest:], tile[:rest]], axis=0).astype(BF16))
        c_ref[s] = jnp.concatenate(tiles, axis=1)[:, :count]


def load_kernel(
    conc_hbm, vel_hbm, type_hbm, table_hbm, inlet_hbm, x_ref, vel_ref, type_ref, table_ref, inlet_ref, right_ref, left_ref,
    near_ref, far_ref, sems, small_sems,
):
    species, tiles_n, levels, dofs, _ = x_ref.shape
    trace = right_ref.shape[0]
    stride = dofs // trace
    small = ((vel_hbm, vel_ref), (type_hbm, type_ref), (table_hbm, table_ref), (inlet_hbm, inlet_ref))
    small = [pltpu.make_async_copy(*ends, small_sems.at[i]) for i, ends in enumerate(small)]
    copies = []
    small[0].start()
    for i in [0, tiles_n - 1, *range(1, tiles_n - 1)]:
        for s in range(species):
            block = conc_hbm.at[s, :, :, pl.ds(i * LANES, LANES)]
            copies.append(pltpu.make_async_copy(block, x_ref.at[s, i], sems.at[s * tiles_n + i]))
            copies[-1].start()
    for copy in small[1:]:
        copy.start()
    small[0].wait()
    lane = lane_index((levels, LANES))
    on_diag = lane % (LANES // species) == lax.broadcasted_iota(jnp.int32, lane.shape, 0)
    face = jnp.broadcast_to(vel_ref[:, :1], (levels, LANES))
    face = jnp.sum(jnp.where(on_diag, face, 0.0), axis=0, keepdims=True)
    left_ref[trace:] = jnp.broadcast_to(face, (left_ref.shape[0] - trace, LANES))
    for copy in copies[: 2 * species]:
        copy.wait()
    lane = lane_index((trace, LANES))
    right = jnp.zeros((trace, LANES), F32)
    left = jnp.zeros((trace, LANES), F32)
    for s in range(species):
        for l in range(levels):
            p = pair_lane(s, l, species)
            last = x_ref[s, tiles_n - 1, l, pl.ds(stride - 1, trace, stride=stride), :]
            first = x_ref[s, 0, l, pl.ds(0, trace, stride=stride), :]
            right = jnp.where(lane == p, pltpu.roll(last, (p + 1) % LANES, 1), right)
            left = jnp.where(lane == p, pltpu.roll(first, p, 1) if p else first, left)
    right_ref[...] = right
    left_ref[:trace] = left
    is_even = lax.axis_index("lat") % 2 == 0
    near_ref[:trace] = jnp.where(is_even, right, left)
    far_ref[:trace] = jnp.where(is_even, left, right)
    near_ref[trace:] = left_ref[trace:]
    far_ref[trace:] = left_ref[trace:]
    for copy in copies[2 * species :] + small[1:]:
        copy.wait()


def fill_coefs(coef_ref, small_ref):
    types_n, trace, _, width = coef_ref.shape
    species = small_ref.shape[0]
    which = lane_index((trace, width)) // (width // species)
    for t in range(types_n):
        for j in range(trace):
            value = jnp.broadcast_to(small_ref[0, t, :, j : j + 1], (trace, width))
            for s in range(1, species):
                other = jnp.broadcast_to(small_ref[s, t, :, j : j + 1], (trace, width))
                value = jnp.where(which == s, other, value)
            coef_ref[t, j] = value


def two_levels(trace_in, c2_ref, s, types, trace):
    return pick(mm(c2_ref[s], stacked_parts(trace_in)), types, trace)


def one_level(trace_in, c1_ref, s, types, trace):
    return pick(mm(c1_ref[s], stacked_parts(trace_in)), types, trace)


def inner_kernel(
    x_ref, vel_ref, type_ref, table_ref, inlet_ref, source_hbm, mid_top_ref, offset_ref, a_top_ref, c1_ref, c2_ref,
    small_ref, coef_ref, source_ref, store_sems,
):
    species, levels, tiles_n, dofs, _ = source_ref.shape
    columns = tiles_n * LANES
    trace = inlet_ref.shape[1]
    types_n = small_ref.shape[1]
    stride = dofs // trace
    fill_top_tables(table_ref, a_top_ref, c1_ref, c2_ref, small_ref, coef_ref)
    lane = lane_index((trace, columns))
    zero, three = pl.ds(0, trace, stride=stride), pl.ds(stride - 1, trace, stride=stride)
    stores = []
    tops = [[] for _ in range(species)]
    traces = []
    start = (lax.axis_index("flow") == 0).astype(F32)
    for l in range(levels):
        velocity = jnp.broadcast_to(vel_ref[l : l + 1], (trace, columns))
        plus = jnp.where(lane > 0, jnp.maximum(velocity, 0.0), 0.0)
        minus = jnp.minimum(velocity, 0.0)
        types = jnp.broadcast_to(type_ref[l : l + 1], (8, columns))
        for s in range(species):
            views = [x_ref.at[s, i, l] for i in range(tiles_n)]
            low = jnp.concatenate([view[zero, :] for view in views], axis=1)
            high = jnp.concatenate([view[three, :] for view in views], axis=1)
            flux = plus * pltpu.roll(high, 1, 1) + minus * low
            out = jnp.where(lane == columns - 1, 0.0, pltpu.roll(flux, columns - 1, 1))
            low, high = low + flux, high - out
            for i, view in enumerate(views):
                source_ref[s, l, i] = view[...]
                source_ref[s, l, i, zero, :] = low[:, i * LANES : (i + 1) * LANES]
                source_ref[s, l, i, three, :] = high[:, i * LANES : (i + 1) * LANES]
            source = jnp.concatenate([source_ref[s, l, i] for i in range(tiles_n)], axis=1)
            top = pick(mm(a_top_ref[s], stacked_parts(source)), types, trace)
            tops[s].append(top)
            mid_top_ref[s, l] = top[:, LANES : columns - LANES]
        if l % 2:
            below = jnp.broadcast_to(type_ref[l - 1 : l], (8, columns))
            both = below * types_n + types
            for s in range(species):
                lower, upper = tops[s][-2:]
                if l == 1:
                    traces.append(inlet_ref[s] * start)
                added = one_level(lower, c1_ref, s, types, trace) + upper
                traces[s] = two_levels(traces[s], c2_ref, s, both, trace) + added
        if (l + 1) % (levels // 2) == 0:
            part = pl.ds(l + 1 - levels // 2, levels // 2)
            for s in range(species):
                ends = source_ref.at[s, part], source_hbm.at[s, part]
                stores.append(pltpu.make_async_copy(*ends, store_sems.at[len(stores)]))
                stores[-1].start()
    for s in range(species):
        offset_ref[s] = traces[s]
    for copy in stores:
        copy.wait()


def trace_step(state, types, coef_ref):
    types_n, trace = coef_ref.shape[:2]
    chosen = [types == float(t) for t in range(1, types_n)]
    terms = []
    for j in range(trace):
        coef = coef_ref[0, j]
        for t in range(1, types_n):
            coef = jnp.where(chosen[t - 1], coef_ref[t, j], coef)
        terms.append(coef * state[j : j + 1])
    return summed(terms)


def halo_kernel(
    offset_ref, type_ref, a_top_ref, coef_ref, own_right_ref, own_left_ref, near_ref, far_ref,
    send_ref, flux_ref, delta_ref,
):
    species, trace, columns = offset_ref.shape
    levels = type_ref.shape[0]
    dofs = delta_ref.shape[0]
    stride = dofs // trace
    lat, lat_n = lax.axis_index("lat"), lax.axis_size("lat")
    has_left = (lat > 0).astype(F32)
    has_right = (lat < lat_n - 1).astype(F32)
    far_edge = LANES // species // 2

    def face(ref):
        return jnp.broadcast_to(ref[trace : trace + 1], (trace, LANES))

    is_even = lat % 2 == 0
    from_left = jnp.where(is_even, far_ref[:trace], near_ref[:trace])
    from_right = jnp.where(is_even, near_ref[:trace], far_ref[:trace])
    coming = jnp.maximum(face(own_left_ref), 0.0) * from_left * has_left
    velocity = jnp.where(is_even, face(near_ref), face(far_ref))
    leaving = jnp.maximum(velocity, 0.0) * own_right_ref[...]
    leaving = -(leaving + jnp.minimum(velocity, 0.0) * from_right) * has_right
    flux_ref[0] = coming
    flux_ref[1] = leaving
    lane = lane_index((trace, LANES))
    within = lane % (LANES // species)
    near, far = within < levels, (within >= far_edge) & (within < far_edge + levels)
    delta_ref[...] = jnp.zeros((dofs, LANES), F32)
    delta_ref[pl.ds(0, trace, stride=stride), :] = jnp.where(near, coming, 0.0)
    delta_ref[pl.ds(stride - 1, trace, stride=stride), :] = jnp.where(
        far, pltpu.roll(leaving, far_edge, 1), 0.0
    )
    types = type_ref[...].astype(F32)
    sub = lax.broadcasted_iota(jnp.int32, (levels, LANES), 0)
    spot = lane_index((levels, LANES)) % (LANES // species)
    here = jnp.where(spot == sub, jnp.broadcast_to(types[:, :1], (levels, LANES)), 0.0)
    there = jnp.broadcast_to(types[:, columns - 1 :], (levels, LANES))
    here = here + jnp.where(spot == sub + far_edge, there, 0.0)
    edge_types = jnp.broadcast_to(jnp.sum(here, axis=0, keepdims=True), (trace, LANES))
    parts = stacked_parts(delta_ref[...])
    added = pick(mm(a_top_ref[0], parts), edge_types[:8], trace)
    for s in range(1, species):
        other = pick(mm(a_top_ref[s], parts), edge_types[:8], trace)
        added = jnp.where(lane < s * (LANES // species), added, other)
    state = added
    for l in range(1, levels):
        state = trace_step(state, pltpu.roll(edge_types, LANES - l, 1), coef_ref)
        state = state + pltpu.roll(added, LANES - l, 1)
    traces = []
    for s in range(species):
        at = pair_lane(s, 0, species)
        first = pltpu.roll(state, LANES - at, 1) if at else state
        last = pltpu.roll(state, LANES - 1 - at - far_edge, 1)
        first = offset_ref[s, :, :LANES] + jnp.where(lane == 0, first, 0.0)
        last = offset_ref[s, :, columns - LANES :] + jnp.where(lane == LANES - 1, last, 0.0)
        traces.append(jnp.concatenate([first, offset_ref[s, :, LANES : columns - LANES], last], axis=1))
    width = send_ref.shape[2]
    if width == LANES:
        half = width // 2
        low = lane_index((trace, width)) < half
        low_t = lane_index((levels, width)) < half
        for k in range(columns // width):
            a, b = (traces[s][:, k * width : (k + 1) * width] for s in (0, 1))
            t = types[:, k * width : (k + 1) * width]
            swapped = pltpu.roll(t, half, 1)
            send_ref[2 * k, :trace] = jnp.where(low, a, pltpu.roll(b, half, 1))
            send_ref[2 * k + 1, :trace] = jnp.where(low, pltpu.roll(a, half, 1), b)
            send_ref[2 * k, trace:] = jnp.where(low_t, t, swapped)
            send_ref[2 * k + 1, trace:] = jnp.where(low_t, swapped, t)
    else:
        for s in range(species):
            send_ref[s, :trace] = traces[s]
            send_ref[s, trace:] = types


def rest_kernel(
    source_hbm, flux_ref, type_ref, a_top_ref, table_ref, small_ref, rest_ref, edge_top_ref, c_ref, coef_ref, a_rest_ref,
    source_ref, sems,
):
    species, levels, tiles_n, dofs, _ = source_ref.shape
    columns = tiles_n * LANES
    rest = rest_ref.shape[2]
    trace = dofs - rest
    stride = dofs // trace
    copies = []
    for h in range(2):
        for s in range(species):
            part = pl.ds(h * (levels // 2), levels // 2)
            ends = source_hbm.at[s, part], source_ref.at[s, part]
            copies.append(pltpu.make_async_copy(*ends, sems.at[len(copies)]))
            copies[-1].start()
    fill_late_tables(table_ref, a_rest_ref, c_ref)
    if len(coef_ref.shape) == 2:
        fill_rows(coef_ref, small_ref)
    else:
        fill_coefs(coef_ref, small_ref)
    lane = lane_index((trace, LANES))
    zero, three = pl.ds(0, trace, stride=stride), pl.ds(stride - 1, trace, stride=stride)
    for l in range(levels):
        types = jnp.broadcast_to(type_ref[l : l + 1], (8, columns))
        edge_types = jnp.concatenate([types[:, :LANES], types[:, columns - LANES :]], axis=1)
        if l % (levels // 2) == 0:
            for s in range(species):
                copies[(l // (levels // 2)) * species + s].wait()
        for s in range(species):
            p = pair_lane(s, l, species)
            first = pltpu.roll(flux_ref[0], (LANES - p) % LANES, 1)
            last = pltpu.roll(flux_ref[1], LANES - 1 - p, 1)
            end = tiles_n - 1
            low, high = source_ref[s, l, 0, zero, :], source_ref[s, l, end, three, :]
            source_ref[s, l, 0, zero, :] = low + jnp.where(lane == 0, first, 0.0)
            source_ref[s, l, end, three, :] = high + jnp.where(lane == LANES - 1, last, 0.0)
            parts = stacked_parts(jnp.concatenate([source_ref[s, l, i] for i in range(tiles_n)], axis=1))
            rest_ref[s, l] = pick(mm(a_rest_ref[s], parts), types, rest)
            outer = jnp.concatenate([parts[:, :LANES], parts[:, columns - LANES :]], axis=1)
            edge_top_ref[s, l] = pick(mm(a_top_ref[s], outer), edge_types, trace)


def fill_rows(rows_ref, small_ref):
    species, types_n, trace, _ = small_ref.shape
    count = species * types_n
    lane = lane_index((trace, LANES))
    for j in range(trace):
        block = jnp.zeros((trace, LANES), F32)
        for t in range(types_n):
            for s in range(species):
                value = jnp.broadcast_to(small_ref[s, t, :, j : j + 1], (trace, LANES))
                block = jnp.where(lane % count == t * species + s, value, block)
        high, left = high_low(block)
        middle, low = high_low(left)
        block = jnp.where(lane < count, high, jnp.where(lane < 2 * count, middle, low))
        rows_ref[j * trace : (j + 1) * trace] = block.astype(BF16)[:, : 3 * count]


def owner_rows_kernel(species, rows_ref, got_ref, out_ref, coef_ref):
    slabs, _, width = got_ref.shape
    trace = out_ref.shape[1]
    levels = got_ref.shape[1] - trace
    depth = rows_ref.shape[1]
    count = depth // 3
    row = (lax.broadcasted_iota(jnp.int32, (depth, width), 0) % count).astype(F32)
    which = (lane_index((depth, width)) // (width // species)).astype(F32)

    def select(g):
        hot = []
        for l in range(levels):
            types = jnp.broadcast_to(got_ref[g, trace + l : trace + l + 1], (depth, width))
            hot.append(jnp.where(types * species + which == row, 1.0, 0.0).astype(BF16))
        coefs = mm(rows_ref[...], jnp.concatenate(hot, axis=1))
        for l in range(levels):
            coef_ref[g % 2, l] = coefs[:, l * width : (l + 1) * width]

    out_ref[0] = jnp.zeros((trace, width), F32)
    state = got_ref[0, :trace]
    select(1)
    for g in range(1, slabs - 1):
        out_ref[g] = state
        if g + 1 < slabs - 1:
            select(g + 1)
        for l in range(levels):
            coefs = [coef_ref[g % 2, l, j * trace : (j + 1) * trace] for j in range(trace)]
            state = summed([coef * state[j : j + 1] for j, coef in enumerate(coefs)])
        state = state + got_ref[g, :trace]
    out_ref[slabs - 1] = state


def owner_kernel(coef_ref, got_ref, out_ref):
    slabs, _, width = got_ref.shape
    trace = coef_ref.shape[1]
    levels = got_ref.shape[1] - trace
    out_ref[0] = jnp.zeros((trace, width), F32)

    def slab(g, state):
        out_ref[g] = state
        for l in range(levels):
            types = jnp.broadcast_to(got_ref[g, trace + l : trace + l + 1], (trace, width))
            state = trace_step(state, types, coef_ref)
        return state + got_ref[g, :trace]

    last = lax.fori_loop(1, slabs - 1, slab, got_ref[0, :trace])
    out_ref[slabs - 1] = last


def final_kernel(
    mid_top_ref, edge_top_ref, rest_ref, type_ref, inlet_ref, c_ref, c1_ref, c2_ref, got_ref, out_hbm, o_ref, sems
):
    species, levels, rest, columns = rest_ref.shape
    trace = inlet_ref.shape[1]
    types_n = c_ref.shape[2] // (3 * trace)
    width = got_ref.shape[2]
    is_first = lax.axis_index("flow") == 0
    if width == LANES:
        half = width // 2
        low = lane_index((trace, width)) < half
        tiles = [[], []]
        for k in range(columns // width):
            a, b = got_ref[2 * k], got_ref[2 * k + 1]
            tiles[0].append(jnp.where(low, a, pltpu.roll(b, half, 1)))
            tiles[1].append(jnp.where(low, pltpu.roll(a, half, 1), b))
        received = [jnp.concatenate(t, axis=1) for t in tiles]
    else:
        received = [got_ref[s] for s in range(species)]
    both = range(species)
    inflow = {(0, s): jnp.where(is_first, inlet_ref[s], received[s]) for s in both}
    types = [jnp.broadcast_to(type_ref[l : l + 1], (8, columns)) for l in range(levels)]

    def top(s, l):
        edge = edge_top_ref[s, l]
        return jnp.concatenate([edge[:, :LANES], mid_top_ref[s, l], edge[:, LANES:]], axis=1)

    added = {}
    for l in range(0, levels - 2, 2):
        for s in both:
            added[l, s] = one_level(top(s, l), c1_ref, s, types[l + 1], trace) + top(s, l + 1)
    copies = []

    def solve(l):
        masks = masks_of(type_ref, l, types_n, trace)
        for s in both:
            moved = mm(c_ref[s], masked_parts(inflow[l, s], masks))
            outflow = moved[:trace] + top(s, l)
            if l % 2 == 0:
                inflow[l + 1, s] = outflow
            o_ref[s, l, rest:] = outflow.astype(BF16)
            o_ref[s, l, :rest] = (moved[trace:] + rest_ref[s, l]).astype(BF16)
            copies.append(pltpu.make_async_copy(o_ref.at[s, l], out_hbm.at[s, l], sems.at[s * levels + l]))
            copies[-1].start()

    for l in range(0, levels, 2):
        if l + 2 < levels:
            for s in both:
                ahead = two_levels(inflow[l, s], c2_ref, s, types[l] * types_n + types[l + 1], trace)
                inflow[l + 2, s] = ahead + added[l, s]
        if l:
            solve(l - 1)
        solve(l)
    solve(levels - 1)
    for copy in copies:
        copy.wait()


def on_device(conc_old, lat_velocity, elem_type, inlet_trace, solve_table):
    species, levels, dofs, columns = conc_old.shape
    types_n = solve_table.shape[1]
    trace = inlet_trace.shape[1]
    flow_n = lax.axis_size("flow")
    lat_n = lax.axis_size("lat")
    pairs = species * levels
    tiles = columns // LANES
    inner = columns - 2 * LANES
    rest = dofs - trace

    def shape(dims, kind=F32):
        return jax.ShapeDtypeStruct(dims, kind)

    def held(dims, kind=F32):
        return pltpu.VMEM(dims, kind)

    def far(array):
        return pltpu.with_memory_space_constraint(array, pltpu.HBM)

    def cost(rows, count):
        flops = 2 * 3 * types_n * rows * dofs * count * pairs
        return pl.CostEstimate(
            flops=flops, bytes_accessed=8 * pairs * dofs * columns, transcendentals=0
        )

    x, velocity, types, table, inlet, right, left, near, far_side = pl.pallas_call(
        load_kernel,
        out_shape=(
            held((species, tiles, levels, dofs, LANES)),
            held(lat_velocity.shape),
            held(elem_type.shape, elem_type.dtype),
            held(solve_table.shape),
            held(inlet_trace.shape),
            held((trace, LANES)),
            held((trace + 8, LANES)),
            shape((trace + 8, LANES)),
            shape((trace + 8, LANES)),
        ),
        in_specs=[HBM] * 5,
        out_specs=(VMEM,) * 9,
        scratch_shapes=[pltpu.SemaphoreType.DMA((species * tiles,)), pltpu.SemaphoreType.DMA((4,))],
        compiler_params=PARAMS,
        name="load_edges",
    )(far(conc_old), far(lat_velocity), far(elem_type), far(solve_table), far(inlet_trace))
    assert lat_n % 2 == 0
    near_got = lax.ppermute(near, "lat", [(i, i ^ 1) for i in range(lat_n)])
    swap = [(i, (i - 1) % lat_n if i % 2 == 0 else (i + 1) % lat_n) for i in range(lat_n)]
    swap = [(i, j) for i, j in swap if abs(i - j) == 1]
    far_got = lax.ppermute(far_side, "lat", swap)


    source_shape = (species, levels, tiles, dofs, LANES)
    source, mid_top, offset, a_top, c_one, c_two, small, coef = pl.pallas_call(
        inner_kernel,
        out_shape=(
            pltpu.HBM(source_shape, F32),
            held((species, levels, trace, inner)),
            held((species, trace, columns)),
            held((species, types_n * trace, 3 * dofs), BF16),
            held((species, types_n * trace, 3 * trace), BF16),
            held((species, types_n * types_n * trace, 3 * trace), BF16),
            held((species, types_n, trace, trace)),
            held((types_n, trace, trace, LANES)),
        ),
        in_specs=[VMEM] * 5,
        out_specs=(HBM,) + (VMEM,) * 7,
        scratch_shapes=[pltpu.VMEM(source_shape, F32), pltpu.SemaphoreType.DMA((2 * species,))],
        compiler_params=PARAMS,
        cost_estimate=cost(dofs, columns),
        name="inner_sources",
    )(x, velocity, types, table, inlet)

    packed = 2 * columns == LANES * flow_n and species == 2
    send_shape = (flow_n, trace + levels, LANES) if packed else (species, trace + levels, columns)
    send, flux = pl.pallas_call(
        halo_kernel,
        out_shape=(shape(send_shape), held((2, trace, LANES))),
        in_specs=[VMEM] * 8,
        out_specs=(VMEM, VMEM),
        scratch_shapes=[pltpu.VMEM((dofs, LANES), F32)],
        compiler_params=PARAMS,
        name="halo_offsets",
    )(offset, types, a_top, coef, right, left, near_got, far_got)
    part = columns // flow_n
    if not packed:
        send = send.reshape(species, trace + levels, flow_n, part)
        send = send.transpose(2, 1, 0, 3).reshape(flow_n, trace + levels, species * part)
    got = lax.all_to_all(send, "flow", 0, 0, tiled=True)

    if packed:
        owner_shape = held((trace * trace, 3 * types_n * species), BF16)
        owner, owner_scratch = functools.partial(owner_rows_kernel, species), [pltpu.VMEM((2, levels, trace * trace, LANES), F32)]
    else:
        owner_shape = held((types_n, trace, trace, species * part))
        owner, owner_scratch = owner_kernel, []
    rest_terms, edge_top, c_all, owner_coef = pl.pallas_call(
        rest_kernel,
        out_shape=(
            held((species, levels, rest, columns)),
            held((species, levels, trace, 2 * LANES)),
            held((species, dofs, 3 * types_n * trace), BF16),
            owner_shape,
        ),
        in_specs=[HBM] + [VMEM] * 5,
        out_specs=(VMEM,) * 4,
        scratch_shapes=[
            pltpu.VMEM((species, types_n * rest, 3 * dofs), BF16),
            pltpu.VMEM(source_shape, F32),
            pltpu.SemaphoreType.DMA((2 * species,)),
        ],
        compiler_params=PARAMS,
        cost_estimate=cost(rest, columns),
        name="rest_sources",
    )(far(source), flux, types, a_top, table, small)
    back = pl.pallas_call(
        owner,
        scratch_shapes=owner_scratch,
        out_shape=shape((flow_n, trace, species * part)),
        in_specs=[VMEM, VMEM],
        out_specs=VMEM,
        compiler_params=PARAMS,
        name="owner_sweep",
    )(owner_coef, got)
    traces = lax.all_to_all(back, "flow", 0, 0, tiled=True)
    if not packed:
        traces = traces.reshape(flow_n, trace, species, part)
        traces = traces.transpose(2, 1, 0, 3).reshape(species, trace, columns)

    return pl.pallas_call(
        final_kernel,
        out_shape=shape(conc_old.shape, BF16),
        in_specs=[VMEM] * 9,
        out_specs=HBM,
        scratch_shapes=[
            pltpu.VMEM(conc_old.shape, BF16),
            pltpu.SemaphoreType.DMA((pairs,)),
        ],
        compiler_params=PARAMS,
        name="final_sweep",
    )(mid_top, edge_top, rest_terms, types, inlet, c_all, c_one, c_two, traces)


def solution(mesh):
    in_specs = (
        P(None, "flow", None, "lat"),
        P("flow", "lat"),
        P("flow", "lat"),
        P(None, None, "lat"),
        P(),
    )
    out_specs = P(None, "flow", None, "lat")
    return jax.shard_map(
        on_device, mesh=mesh, in_specs=in_specs, out_specs=out_specs, check_vma=False
    )
```

```python
import functools

import jax
import jax.numpy as jnp
from jax import lax
from jax.experimental import pallas as pl
from jax.experimental.pallas import tpu as pltpu
from jax.sharding import PartitionSpec as P

F32 = jnp.float32
BF16 = jnp.bfloat16
VMEM = pl.BlockSpec(memory_space=pltpu.VMEM)
HBM = pl.BlockSpec(memory_space=pltpu.HBM)
LANES = 128
PARAMS = pltpu.CompilerParams(vmem_limit_bytes=20 << 20)


def lane_index(shape):
    return lax.broadcasted_iota(jnp.int32, shape, len(shape) - 1)


def split(x):
    hi = x.astype(BF16)
    return hi, (x - hi.astype(F32)).astype(BF16)


def stacked_parts(x):
    hi, lo = split(x)
    return jnp.concatenate([hi, lo, hi], axis=0)


def pick(per_type, types, rows):
    columns = per_type.shape[1]
    grid = per_type.reshape(-1, rows // 8, 8, columns)
    out = grid[0]
    for t in range(1, grid.shape[0]):
        out = jnp.where((types == t)[None], grid[t], out)
    return out.reshape(rows, columns)


def masked_parts(x, masks):
    hi, lo = split(x)
    parts = []
    for mask in masks:
        his = hi * mask
        parts += [his, lo * mask, his]
    return jnp.concatenate(parts, axis=0)


def masks_of(type_ref, level, types_n, rows):
    types = jnp.broadcast_to(type_ref[level : level + 1], (rows, type_ref.shape[1]))
    return [jnp.where(types == t, 1.0, 0.0).astype(BF16) for t in range(types_n)]


def mm(a, b):
    return jnp.dot(a, b, preferred_element_type=F32)


def pair_lane(s, l, species):
    return s * (LANES // species) + l


def placed(pieces, rows):
    lane = lane_index((rows, LANES))
    tile = jnp.zeros((rows, LANES), F32)
    for array, source, target, count in pieces:
        moved = pltpu.roll(array, (target - source) % LANES, 1) if target != source else array
        tile = jnp.where((lane >= target) & (lane < target + count), moved, tile)
    return tile


def summed(terms):
    while len(terms) > 1:
        terms = [a + b for a, b in zip(terms[::2], terms[1::2])]
    return terms[0]


def high_low(x):
    hi = x.astype(BF16).astype(F32)
    return hi, x - hi


def table_parts(table_ref, s, t):
    dofs, wide_n = table_ref.shape[2:]
    return high_low(jnp.concatenate([table_ref[s, t], jnp.zeros((dofs, LANES - wide_n), F32)], axis=1))


def source_rows(hi, lo, dofs):
    twice = jnp.where(lane_index(hi.shape) < dofs, hi, pltpu.roll(hi, dofs, 1))
    return jnp.concatenate([twice, lo[:, :dofs]], axis=1).astype(BF16)


def fill_top_tables(table_ref, a_top_ref, c1_ref, c2_ref, small_ref, coef_ref):
    species, types_n, dofs, _ = table_ref.shape
    trace = small_ref.shape[2]
    rest = dofs - trace
    share = LANES // species
    below = []
    for s in range(species):
        tops, single = [], []
        for t in range(types_n):
            hi, lo = (part[rest:] for part in table_parts(table_ref, s, t))
            small_ref[s, t] = table_ref[s, t, rest:, dofs:]
            tops.append(source_rows(hi, lo, dofs))
            pieces = [(hi, dofs, 0, trace), (hi, dofs, trace, trace), (lo, dofs, 2 * trace, trace)]
            single.append(placed(pieces, trace))
            below.append((hi + lo, dofs, s * share + t * trace, trace))
        a_top_ref[s] = jnp.concatenate(tops, axis=0)
        c1_ref[s] = jnp.concatenate(single, axis=0).astype(BF16)[:, : 3 * trace]
    fill_coefs(coef_ref, small_ref)
    below = placed(below, trace)
    products = []
    for t in range(types_n):
        terms = [coef_ref[t, k] * below[k : k + 1] for k in range(trace)]
        products.append(high_low(summed(terms)))
    for s in range(species):
        double = []
        for t in range(types_n):
            at = s * share + t * trace
            for hi, lo in products:
                pieces = [(hi, at, 0, trace), (hi, at, trace, trace), (lo, at, 2 * trace, trace)]
                double.append(placed(pieces, trace))
        c2_ref[s] = jnp.concatenate(double, axis=0).astype(BF16)[:, : 3 * trace]


def fill_late_tables(table_ref, a_rest_ref, c_ref):
    species, types_n, dofs, _ = table_ref.shape
    count = c_ref.shape[2]
    trace = count // (3 * types_n)
    rest = dofs - trace
    for s in range(species):
        parts = [table_parts(table_ref, s, t) for t in range(types_n)]
        a_rest_ref[s] = jnp.concatenate([source_rows(hi[:rest], lo[:rest], dofs) for hi, lo in parts], axis=0)
        tiles = []
        for start in range(0, count, LANES):
            pieces = []
            for at in range(start, min(count, start + LANES), trace):
                k = at // trace
                pieces.append((parts[k // 3][(0, 0, 1)[k % 3]], dofs, at - start, trace))
            tile = placed(pieces, dofs)
            tiles.append(jnp.concatenate([tile[rest:], tile[:rest]], axis=0).astype(BF16))
        c_ref[s] = jnp.concatenate(tiles, axis=1)[:, :count]


def load_kernel(
    conc_hbm, vel_hbm, type_hbm, table_hbm, inlet_hbm, x_ref, vel_ref, type_ref, table_ref, inlet_ref, right_ref, left_ref,
    near_ref, far_ref, sems, small_sems,
):
    species, tiles_n, levels, dofs, _ = x_ref.shape
    trace = right_ref.shape[0]
    stride = dofs // trace
    small = ((vel_hbm, vel_ref), (type_hbm, type_ref), (table_hbm, table_ref), (inlet_hbm, inlet_ref))
    small = [pltpu.make_async_copy(*ends, small_sems.at[i]) for i, ends in enumerate(small)]
    copies = []
    small[0].start()
    for i in [0, tiles_n - 1, *range(1, tiles_n - 1)]:
        for s in range(species):
            block = conc_hbm.at[s, :, :, pl.ds(i * LANES, LANES)]
            copies.append(pltpu.make_async_copy(block, x_ref.at[s, i], sems.at[s * tiles_n + i]))
            copies[-1].start()
    for copy in small[1:]:
        copy.start()
    small[0].wait()
    lane = lane_index((levels, LANES))
    on_diag = lane % (LANES // species) == lax.broadcasted_iota(jnp.int32, lane.shape, 0)
    face = jnp.broadcast_to(vel_ref[:, :1], (levels, LANES))
    face = jnp.sum(jnp.where(on_diag, face, 0.0), axis=0, keepdims=True)
    left_ref[trace:] = jnp.broadcast_to(face, (left_ref.shape[0] - trace, LANES))
    for copy in copies[: 2 * species]:
        copy.wait()
    lane = lane_index((trace, LANES))
    right = jnp.zeros((trace, LANES), F32)
    left = jnp.zeros((trace, LANES), F32)
    for s in range(species):
        for l in range(levels):
            p = pair_lane(s, l, species)
            last = x_ref[s, tiles_n - 1, l, pl.ds(stride - 1, trace, stride=stride), :]
            first = x_ref[s, 0, l, pl.ds(0, trace, stride=stride), :]
            right = jnp.where(lane == p, pltpu.roll(last, (p + 1) % LANES, 1), right)
            left = jnp.where(lane == p, pltpu.roll(first, p, 1) if p else first, left)
    right_ref[...] = right
    left_ref[:trace] = left
    is_even = lax.axis_index("lat") % 2 == 0
    near_ref[:trace] = jnp.where(is_even, right, left)
    far_ref[:trace] = jnp.where(is_even, left, right)
    near_ref[trace:] = left_ref[trace:]
    far_ref[trace:] = left_ref[trace:]
    for copy in copies[2 * species :] + small[1:]:
        copy.wait()


def fill_coefs(coef_ref, small_ref):
    types_n, trace, _, width = coef_ref.shape
    species = small_ref.shape[0]
    which = lane_index((trace, width)) // (width // species)
    for t in range(types_n):
        for j in range(trace):
            value = jnp.broadcast_to(small_ref[0, t, :, j : j + 1], (trace, width))
            for s in range(1, species):
                other = jnp.broadcast_to(small_ref[s, t, :, j : j + 1], (trace, width))
                value = jnp.where(which == s, other, value)
            coef_ref[t, j] = value


def two_levels(trace_in, c2_ref, s, types, trace):
    return pick(mm(c2_ref[s], stacked_parts(trace_in)), types, trace)


def one_level(trace_in, c1_ref, s, types, trace):
    return pick(mm(c1_ref[s], stacked_parts(trace_in)), types, trace)


def inner_kernel(
    x_ref, vel_ref, type_ref, table_ref, inlet_ref, source_hbm, mid_top_ref, offset_ref, a_top_ref, c1_ref, c2_ref,
    small_ref, coef_ref, source_ref, store_sems,
):
    species, levels, tiles_n, dofs, _ = source_ref.shape
    columns = tiles_n * LANES
    trace = inlet_ref.shape[1]
    types_n = small_ref.shape[1]
    stride = dofs // trace
    fill_top_tables(table_ref, a_top_ref, c1_ref, c2_ref, small_ref, coef_ref)
    lane = lane_index((trace, columns))
    zero, three = pl.ds(0, trace, stride=stride), pl.ds(stride - 1, trace, stride=stride)
    stores = []
    tops = [[] for _ in range(species)]
    traces = []
    start = (lax.axis_index("flow") == 0).astype(F32)
    for l in range(levels):
        velocity = jnp.broadcast_to(vel_ref[l : l + 1], (trace, columns))
        plus = jnp.where(lane > 0, jnp.maximum(velocity, 0.0), 0.0)
        minus = jnp.minimum(velocity, 0.0)
        types = jnp.broadcast_to(type_ref[l : l + 1], (8, columns))
        for s in range(species):
            views = [x_ref.at[s, i, l] for i in range(tiles_n)]
            low = jnp.concatenate([view[zero, :] for view in views], axis=1)
            high = jnp.concatenate([view[three, :] for view in views], axis=1)
            flux = plus * pltpu.roll(high, 1, 1) + minus * low
            out = jnp.where(lane == columns - 1, 0.0, pltpu.roll(flux, columns - 1, 1))
            low, high = low + flux, high - out
            for i, view in enumerate(views):
                source_ref[s, l, i] = view[...]
                source_ref[s, l, i, zero, :] = low[:, i * LANES : (i + 1) * LANES]
                source_ref[s, l, i, three, :] = high[:, i * LANES : (i + 1) * LANES]
            source = jnp.concatenate([source_ref[s, l, i] for i in range(tiles_n)], axis=1)
            top = pick(mm(a_top_ref[s], stacked_parts(source)), types, trace)
            tops[s].append(top)
            mid_top_ref[s, l] = top[:, LANES : columns - LANES]
        if l % 2:
            below = jnp.broadcast_to(type_ref[l - 1 : l], (8, columns))
            both = below * types_n + types
            for s in range(species):
                lower, upper = tops[s][-2:]
                if l == 1:
                    traces.append(inlet_ref[s] * start)
                added = one_level(lower, c1_ref, s, types, trace) + upper
                traces[s] = two_levels(traces[s], c2_ref, s, both, trace) + added
        if (l + 1) % (levels // 2) == 0:
            part = pl.ds(l + 1 - levels // 2, levels // 2)
            for s in range(species):
                ends = source_ref.at[s, part], source_hbm.at[s, part]
                stores.append(pltpu.make_async_copy(*ends, store_sems.at[len(stores)]))
                stores[-1].start()
    for s in range(species):
        offset_ref[s] = traces[s]
    for copy in stores:
        copy.wait()


def trace_step(state, types, coef_ref):
    types_n, trace = coef_ref.shape[:2]
    chosen = [types == float(t) for t in range(1, types_n)]
    terms = []
    for j in range(trace):
        coef = coef_ref[0, j]
        for t in range(1, types_n):
            coef = jnp.where(chosen[t - 1], coef_ref[t, j], coef)
        terms.append(coef * state[j : j + 1])
    return summed(terms)


def halo_kernel(
    offset_ref, type_ref, a_top_ref, coef_ref, own_right_ref, own_left_ref, near_ref, far_ref,
    send_ref, flux_ref, delta_ref,
):
    species, trace, columns = offset_ref.shape
    levels = type_ref.shape[0]
    dofs = delta_ref.shape[0]
    stride = dofs // trace
    lat, lat_n = lax.axis_index("lat"), lax.axis_size("lat")
    has_left = (lat > 0).astype(F32)
    has_right = (lat < lat_n - 1).astype(F32)
    far_edge = LANES // species // 2

    def face(ref):
        return jnp.broadcast_to(ref[trace : trace + 1], (trace, LANES))

    is_even = lat % 2 == 0
    from_left = jnp.where(is_even, far_ref[:trace], near_ref[:trace])
    from_right = jnp.where(is_even, near_ref[:trace], far_ref[:trace])
    coming = jnp.maximum(face(own_left_ref), 0.0) * from_left * has_left
    velocity = jnp.where(is_even, face(near_ref), face(far_ref))
    leaving = jnp.maximum(velocity, 0.0) * own_right_ref[...]
    leaving = -(leaving + jnp.minimum(velocity, 0.0) * from_right) * has_right
    flux_ref[0] = coming
    flux_ref[1] = leaving
    lane = lane_index((trace, LANES))
    within = lane % (LANES // species)
    near, far = within < levels, (within >= far_edge) & (within < far_edge + levels)
    delta_ref[...] = jnp.zeros((dofs, LANES), F32)
    delta_ref[pl.ds(0, trace, stride=stride), :] = jnp.where(near, coming, 0.0)
    delta_ref[pl.ds(stride - 1, trace, stride=stride), :] = jnp.where(
        far, pltpu.roll(leaving, far_edge, 1), 0.0
    )
    types = type_ref[...].astype(F32)
    sub = lax.broadcasted_iota(jnp.int32, (levels, LANES), 0)
    spot = lane_index((levels, LANES)) % (LANES // species)
    here = jnp.where(spot == sub, jnp.broadcast_to(types[:, :1], (levels, LANES)), 0.0)
    there = jnp.broadcast_to(types[:, columns - 1 :], (levels, LANES))
    here = here + jnp.where(spot == sub + far_edge, there, 0.0)
    edge_types = jnp.broadcast_to(jnp.sum(here, axis=0, keepdims=True), (trace, LANES))
    parts = stacked_parts(delta_ref[...])
    added = pick(mm(a_top_ref[0], parts), edge_types[:8], trace)
    for s in range(1, species):
        other = pick(mm(a_top_ref[s], parts), edge_types[:8], trace)
        added = jnp.where(lane < s * (LANES // species), added, other)
    state = added
    for l in range(1, levels):
        state = trace_step(state, pltpu.roll(edge_types, LANES - l, 1), coef_ref)
        state = state + pltpu.roll(added, LANES - l, 1)
    traces = []
    for s in range(species):
        at = pair_lane(s, 0, species)
        first = pltpu.roll(state, LANES - at, 1) if at else state
        last = pltpu.roll(state, LANES - 1 - at - far_edge, 1)
        first = offset_ref[s, :, :LANES] + jnp.where(lane == 0, first, 0.0)
        last = offset_ref[s, :, columns - LANES :] + jnp.where(lane == LANES - 1, last, 0.0)
        traces.append(jnp.concatenate([first, offset_ref[s, :, LANES : columns - LANES], last], axis=1))
    width = send_ref.shape[2]
    if width == LANES:
        half = width // 2
        low = lane_index((trace, width)) < half
        low_t = lane_index((levels, width)) < half
        for k in range(columns // width):
            a, b = (traces[s][:, k * width : (k + 1) * width] for s in (0, 1))
            t = types[:, k * width : (k + 1) * width]
            swapped = pltpu.roll(t, half, 1)
            send_ref[2 * k, :trace] = jnp.where(low, a, pltpu.roll(b, half, 1))
            send_ref[2 * k + 1, :trace] = jnp.where(low, pltpu.roll(a, half, 1), b)
            send_ref[2 * k, trace:] = jnp.where(low_t, t, swapped)
            send_ref[2 * k + 1, trace:] = jnp.where(low_t, swapped, t)
    else:
        for s in range(species):
            send_ref[s, :trace] = traces[s]
            send_ref[s, trace:] = types


def rest_kernel(
    source_hbm, flux_ref, type_ref, a_top_ref, table_ref, small_ref, rest_ref, edge_top_ref, c_ref, coef_ref, a_rest_ref,
    source_ref, sems,
):
    species, levels, tiles_n, dofs, _ = source_ref.shape
    columns = tiles_n * LANES
    rest = rest_ref.shape[2]
    trace = dofs - rest
    stride = dofs // trace
    copies = []
    for h in range(2):
        for s in range(species):
            part = pl.ds(h * (levels // 2), levels // 2)
            ends = source_hbm.at[s, part], source_ref.at[s, part]
            copies.append(pltpu.make_async_copy(*ends, sems.at[len(copies)]))
            copies[-1].start()
    fill_late_tables(table_ref, a_rest_ref, c_ref)
    if len(coef_ref.shape) == 2:
        fill_rows(coef_ref, small_ref)
    else:
        fill_coefs(coef_ref, small_ref)
    lane = lane_index((trace, LANES))
    zero, three = pl.ds(0, trace, stride=stride), pl.ds(stride - 1, trace, stride=stride)
    for l in range(levels):
        types = jnp.broadcast_to(type_ref[l : l + 1], (8, columns))
        edge_types = jnp.concatenate([types[:, :LANES], types[:, columns - LANES :]], axis=1)
        if l % (levels // 2) == 0:
            for s in range(species):
                copies[(l // (levels // 2)) * species + s].wait()
        for s in range(species):
            p = pair_lane(s, l, species)
            first = pltpu.roll(flux_ref[0], (LANES - p) % LANES, 1)
            last = pltpu.roll(flux_ref[1], LANES - 1 - p, 1)
            end = tiles_n - 1
            low, high = source_ref[s, l, 0, zero, :], source_ref[s, l, end, three, :]
            source_ref[s, l, 0, zero, :] = low + jnp.where(lane == 0, first, 0.0)
            source_ref[s, l, end, three, :] = high + jnp.where(lane == LANES - 1, last, 0.0)
            parts = stacked_parts(jnp.concatenate([source_ref[s, l, i] for i in range(tiles_n)], axis=1))
            rest_ref[s, l] = pick(mm(a_rest_ref[s], parts), types, rest)
            outer = jnp.concatenate([parts[:, :LANES], parts[:, columns - LANES :]], axis=1)
            edge_top_ref[s, l] = pick(mm(a_top_ref[s], outer), edge_types, trace)


def fill_rows(rows_ref, small_ref):
    species, types_n, trace, _ = small_ref.shape
    count = species * types_n
    lane = lane_index((trace, LANES))
    for j in range(trace):
        block = jnp.zeros((trace, LANES), F32)
        for t in range(types_n):
            for s in range(species):
                value = jnp.broadcast_to(small_ref[s, t, :, j : j + 1], (trace, LANES))
                block = jnp.where(lane % count == t * species + s, value, block)
        high, left = high_low(block)
        middle, low = high_low(left)
        block = jnp.where(lane < count, high, jnp.where(lane < 2 * count, middle, low))
        rows_ref[j * trace : (j + 1) * trace] = block.astype(BF16)[:, : 3 * count]


def owner_rows_kernel(species, rows_ref, got_ref, out_ref, coef_ref):
    slabs, _, width = got_ref.shape
    trace = out_ref.shape[1]
    levels = got_ref.shape[1] - trace
    depth = rows_ref.shape[1]
    count = depth // 3
    row = (lax.broadcasted_iota(jnp.int32, (depth, width), 0) % count).astype(F32)
    which = (lane_index((depth, width)) // (width // species)).astype(F32)

    def select(g):
        hot = []
        for l in range(levels):
            types = jnp.broadcast_to(got_ref[g, trace + l : trace + l + 1], (depth, width))
            hot.append(jnp.where(types * species + which == row, 1.0, 0.0).astype(BF16))
        coefs = mm(rows_ref[...], jnp.concatenate(hot, axis=1))
        for l in range(levels):
            coef_ref[g % 2, l] = coefs[:, l * width : (l + 1) * width]

    out_ref[0] = jnp.zeros((trace, width), F32)
    state = got_ref[0, :trace]
    select(1)
    for g in range(1, slabs - 1):
        out_ref[g] = state
        if g + 1 < slabs - 1:
            select(g + 1)
        for l in range(levels):
            coefs = [coef_ref[g % 2, l, j * trace : (j + 1) * trace] for j in range(trace)]
            state = summed([coef * state[j : j + 1] for j, coef in enumerate(coefs)])
        state = state + got_ref[g, :trace]
    out_ref[slabs - 1] = state


def owner_kernel(coef_ref, got_ref, out_ref):
    slabs, _, width = got_ref.shape
    trace = coef_ref.shape[1]
    levels = got_ref.shape[1] - trace
    out_ref[0] = jnp.zeros((trace, width), F32)

    def slab(g, state):
        out_ref[g] = state
        for l in range(levels):
            types = jnp.broadcast_to(got_ref[g, trace + l : trace + l + 1], (trace, width))
            state = trace_step(state, types, coef_ref)
        return state + got_ref[g, :trace]

    last = lax.fori_loop(1, slabs - 1, slab, got_ref[0, :trace])
    out_ref[slabs - 1] = last


def final_kernel(
    mid_top_ref, edge_top_ref, rest_ref, type_ref, inlet_ref, c_ref, c1_ref, c2_ref, got_ref, out_hbm, o_ref, sems
):
    species, levels, rest, columns = rest_ref.shape
    trace = inlet_ref.shape[1]
    types_n = c_ref.shape[2] // (3 * trace)
    width = got_ref.shape[2]
    is_first = lax.axis_index("flow") == 0
    if width == LANES:
        half = width // 2
        low = lane_index((trace, width)) < half
        tiles = [[], []]
        for k in range(columns // width):
            a, b = got_ref[2 * k], got_ref[2 * k + 1]
            tiles[0].append(jnp.where(low, a, pltpu.roll(b, half, 1)))
            tiles[1].append(jnp.where(low, pltpu.roll(a, half, 1), b))
        received = [jnp.concatenate(t, axis=1) for t in tiles]
    else:
        received = [got_ref[s] for s in range(species)]
    both = range(species)
    inflow = {(0, s): jnp.where(is_first, inlet_ref[s], received[s]) for s in both}
    types = [jnp.broadcast_to(type_ref[l : l + 1], (8, columns)) for l in range(levels)]

    def top(s, l):
        edge = edge_top_ref[s, l]
        return jnp.concatenate([edge[:, :LANES], mid_top_ref[s, l], edge[:, LANES:]], axis=1)

    added = {}
    for l in range(0, levels - 2, 2):
        for s in both:
            added[l, s] = one_level(top(s, l), c1_ref, s, types[l + 1], trace) + top(s, l + 1)
    copies = []

    def solve(l):
        masks = masks_of(type_ref, l, types_n, trace)
        for s in both:
            moved = mm(c_ref[s], masked_parts(inflow[l, s], masks))
            outflow = moved[:trace] + top(s, l)
            if l % 2 == 0:
                inflow[l + 1, s] = outflow
            o_ref[s, l, rest:] = outflow.astype(BF16)
            o_ref[s, l, :rest] = (moved[trace:] + rest_ref[s, l]).astype(BF16)
            copies.append(pltpu.make_async_copy(o_ref.at[s, l], out_hbm.at[s, l], sems.at[s * levels + l]))
            copies[-1].start()

    for l in range(0, levels, 2):
        if l + 2 < levels:
            for s in both:
                ahead = two_levels(inflow[l, s], c2_ref, s, types[l] * types_n + types[l + 1], trace)
                inflow[l + 2, s] = ahead + added[l, s]
        if l:
            solve(l - 1)
        solve(l)
    solve(levels - 1)
    for copy in copies:
        copy.wait()


def on_device(conc_old, lat_velocity, elem_type, inlet_trace, solve_table):
    species, levels, dofs, columns = conc_old.shape
    types_n = solve_table.shape[1]
    trace = inlet_trace.shape[1]
    flow_n = lax.axis_size("flow")
    lat_n = lax.axis_size("lat")
    pairs = species * levels
    tiles = columns // LANES
    inner = columns - 2 * LANES
    rest = dofs - trace

    def shape(dims, kind=F32):
        return jax.ShapeDtypeStruct(dims, kind)

    def held(dims, kind=F32):
        return pltpu.VMEM(dims, kind)

    def far(array):
        return pltpu.with_memory_space_constraint(array, pltpu.HBM)

    def cost(rows, count):
        flops = 2 * 3 * types_n * rows * dofs * count * pairs
        return pl.CostEstimate(
            flops=flops, bytes_accessed=8 * pairs * dofs * columns, transcendentals=0
        )

    x, velocity, types, table, inlet, right, left, near, far_side = pl.pallas_call(
        load_kernel,
        out_shape=(
            held((species, tiles, levels, dofs, LANES)),
            held(lat_velocity.shape),
            held(elem_type.shape, elem_type.dtype),
            held(solve_table.shape),
            held(inlet_trace.shape),
            held((trace, LANES)),
            held((trace + 8, LANES)),
            shape((trace + 8, LANES)),
            shape((trace + 8, LANES)),
        ),
        in_specs=[HBM] * 5,
        out_specs=(VMEM,) * 9,
        scratch_shapes=[pltpu.SemaphoreType.DMA((species * tiles,)), pltpu.SemaphoreType.DMA((4,))],
        compiler_params=PARAMS,
        name="load_edges",
    )(far(conc_old), far(lat_velocity), far(elem_type), far(solve_table), far(inlet_trace))
    assert lat_n % 2 == 0
    near_got = lax.ppermute(near, "lat", [(i, i ^ 1) for i in range(lat_n)])
    assert flow_n % 2 == 0
    swap = []
    for f in range(flow_n):
        for i in range(lat_n):
            other = i - 1 if i % 2 == 0 else i + 1
            target = f * lat_n + other if 0 <= other < lat_n else (f ^ 1) * lat_n + i
            swap.append((f * lat_n + i, target))
    far_got = lax.ppermute(far_side, ("flow", "lat"), swap)


    source_shape = (species, levels, tiles, dofs, LANES)
    source, mid_top, offset, a_top, c_one, c_two, small, coef = pl.pallas_call(
        inner_kernel,
        out_shape=(
            pltpu.HBM(source_shape, F32),
            held((species, levels, trace, inner)),
            held((species, trace, columns)),
            held((species, types_n * trace, 3 * dofs), BF16),
            held((species, types_n * trace, 3 * trace), BF16),
            held((species, types_n * types_n * trace, 3 * trace), BF16),
            held((species, types_n, trace, trace)),
            held((types_n, trace, trace, LANES)),
        ),
        in_specs=[VMEM] * 5,
        out_specs=(HBM,) + (VMEM,) * 7,
        scratch_shapes=[pltpu.VMEM(source_shape, F32), pltpu.SemaphoreType.DMA((2 * species,))],
        compiler_params=PARAMS,
        cost_estimate=cost(dofs, columns),
        name="inner_sources",
    )(x, velocity, types, table, inlet)

    packed = 2 * columns == LANES * flow_n and species == 2
    send_shape = (flow_n, trace + levels, LANES) if packed else (species, trace + levels, columns)
    send, flux = pl.pallas_call(
        halo_kernel,
        out_shape=(shape(send_shape), held((2, trace, LANES))),
        in_specs=[VMEM] * 8,
        out_specs=(VMEM, VMEM),
        scratch_shapes=[pltpu.VMEM((dofs, LANES), F32)],
        compiler_params=PARAMS,
        name="halo_offsets",
    )(offset, types, a_top, coef, right, left, near_got, far_got)
    part = columns // flow_n
    if not packed:
        send = send.reshape(species, trace + levels, flow_n, part)
        send = send.transpose(2, 1, 0, 3).reshape(flow_n, trace + levels, species * part)
    got = lax.all_to_all(send, "flow", 0, 0, tiled=True)

    if packed:
        owner_shape = held((trace * trace, 3 * types_n * species), BF16)
        owner, owner_scratch = functools.partial(owner_rows_kernel, species), [pltpu.VMEM((2, levels, trace * trace, LANES), F32)]
    else:
        owner_shape = held((types_n, trace, trace, species * part))
        owner, owner_scratch = owner_kernel, []
    rest_terms, edge_top, c_all, owner_coef = pl.pallas_call(
        rest_kernel,
        out_shape=(
            held((species, levels, rest, columns)),
            held((species, levels, trace, 2 * LANES)),
            held((species, dofs, 3 * types_n * trace), BF16),
            owner_shape,
        ),
        in_specs=[HBM] + [VMEM] * 5,
        out_specs=(VMEM,) * 4,
        scratch_shapes=[
            pltpu.VMEM((species, types_n * rest, 3 * dofs), BF16),
            pltpu.VMEM(source_shape, F32),
            pltpu.SemaphoreType.DMA((2 * species,)),
        ],
        compiler_params=PARAMS,
        cost_estimate=cost(rest, columns),
        name="rest_sources",
    )(far(source), flux, types, a_top, table, small)
    back = pl.pallas_call(
        owner,
        scratch_shapes=owner_scratch,
        out_shape=shape((flow_n, trace, species * part)),
        in_specs=[VMEM, VMEM],
        out_specs=VMEM,
        compiler_params=PARAMS,
        name="owner_sweep",
    )(owner_coef, got)
    traces = lax.all_to_all(back, "flow", 0, 0, tiled=True)
    if not packed:
        traces = traces.reshape(flow_n, trace, species, part)
        traces = traces.transpose(2, 1, 0, 3).reshape(species, trace, columns)

    return pl.pallas_call(
        final_kernel,
        out_shape=shape(conc_old.shape, BF16),
        in_specs=[VMEM] * 9,
        out_specs=HBM,
        scratch_shapes=[
            pltpu.VMEM(conc_old.shape, BF16),
            pltpu.SemaphoreType.DMA((pairs,)),
        ],
        compiler_params=PARAMS,
        name="final_sweep",
    )(mid_top, edge_top, rest_terms, types, inlet, c_all, c_one, c_two, traces)


def solution(mesh):
    in_specs = (
        P(None, "flow", None, "lat"),
        P("flow", "lat"),
        P("flow", "lat"),
        P(None, None, "lat"),
        P(),
    )
    out_specs = P(None, "flow", None, "lat")
    return jax.shard_map(
        on_device, mesh=mesh, in_specs=in_specs, out_specs=out_specs, check_vma=False
    )
```
